128 devices in a mesh: obj: 16 (over z, x), scan: 8 (over y, core).
Axes of the slice: x: 4, y: 4, z: 4, core: 2. Of those that a mesh axis runs over, the one named last changes fastest.
Arguments:
- object_tiles: bfloat16 [2, 2, 6144, 384], P(None, None, 'obj'), may hold values from -4 to 4
- probe_modes: float32 [4, 2, 128, 128], replicated, may hold values from -6 to 6
- phase_map: float32 [128, 128], replicated, may hold values from -3.140625 to 3.140625
- amplitudes: float32 [512, 128, 128], P(('obj', 'scan')), may hold values from 0.5 to 3
- offsets: int32 [512, 2], P(('obj', 'scan')), may hold values from 0 to 256
- owners: int32 [512, 1], P(('obj', 'scan')), may hold values from 0 to 15; in each aligned block of 4 rows (0 to 3, 4 to 7, ...) at most 2 rows name the same one
Outputs:
- object_grad: float32 [2, 2, 6144, 384], P(None, None, 'obj')
- probe_grad: float32 [4, 2, 128, 128], replicated
The draws below stay inside these ranges and needn't reach their ends.
Inputs may be any that keep to these rules, and one draw needn't show every extreme that they name: `owners`: in each aligned block of 4 rows (the positions of one device) at most 2 rows name the same tile, and every draw has a block where some tile is named by exactly 2 rows.
All inputs are finite; a program needn't handle non-finite values.
Results may differ from the reference program's by a relative error of at most 0.0015.
Values may be sent and summed in bfloat16 or wider, within the bound.
A program may use at most 128 MiB of HBM per device.

```python
import math
import jax
import jax.numpy as jnp
import numpy as np
from jax import lax

PX = 128
MODES = 4
SLICES = 2
TILE = 384
POS_DEV = 4
CAP = 2
POSITIONS = 512
N_OBJ = 16


def plant(entries, own_key, least, largest):
    longest = entries.shape.index(max(entries.shape))
    spots = []
    for shift in (0, 1):
        where = [jax.random.randint(jax.random.fold_in(own_key, axis), (), 0, length) for axis, length in enumerate(entries.shape)]
        where[longest] = (where[longest] + shift) % entries.shape[longest]
        spots.append(tuple(where))
    return entries.at[spots[0]].set(least).at[spots[1]].set(largest)


def steps_of(rng, extent, pieces, smallest, largest):
    def one(dim, blocks):
        draws = jax.random.uniform(jax.random.fold_in(jax.random.fold_in(rng, 6), dim), (blocks,), jnp.float32, smallest / len(pieces), largest / len(pieces))
        return jnp.repeat(jnp.exp(draws), extent[dim] // blocks).reshape((-1,) + (1,) * (len(extent) - dim - 1))

    factor_of = one(*pieces[0])
    for cut in pieces[1:]:
        factor_of = factor_of * one(*cut)
    return factor_of


def deal_out(key, own, number, rows, count, top, reach, lean):
    ranking = jax.random.permutation(key, count)
    crowded, usual = portions_of(count, rows * top, reach, lean, True), portions_of(count, rows * top, reach, lean, False)
    places = jnp.arange(count)

    def named(sizes, offset_by):
        used = int((sizes > 0).sum())
        fixed = max(1, used // 4)
        moved = fixed + (places - fixed + offset_by * (used - fixed)) % max(1, count - fixed)
        return jnp.zeros((count,), jnp.int32).at[ranking[jnp.where(places < fixed, places, moved)]].set(jnp.asarray(sizes, jnp.int32))

    sizes = jnp.where(number % 4 == 0, named(crowded, number // 4), named(usual, number - number // 4 - 1))
    mixed = jax.random.permutation(jax.random.fold_in(own, 3), count)
    giver, taker = mixed[0:count // 2 * 2:2], mixed[1:count // 2 * 2:2]
    margin = jnp.minimum(sizes[giver] - 1, reach - sizes[taker]) // 2
    margin = jnp.where((giver == ranking[0]) | (taker == ranking[0]) | (sizes[taker] == 0), 0, jnp.maximum(margin, 0))
    moved = jax.random.randint(jax.random.fold_in(own, 4), (count // 2,), 0, 1 << 20) % (margin + 1)
    sizes = sizes.at[giver].add(-moved).at[taker].add(moved)
    labels = jnp.searchsorted(jnp.cumsum(sizes), jnp.arange(rows * top), side="right").astype(jnp.int32)
    grid = labels.reshape(top, rows).T
    grid = grid[jax.random.permutation(jax.random.fold_in(own, 1), rows)]
    offset_by = jax.random.randint(jax.random.fold_in(own, 2), (rows, 1), 0, top)
    return jnp.take_along_axis(grid, (jnp.arange(top)[None, :] + offset_by) % top, axis=1)


def portions_of(number_of, total, limit, slope, full):
    weights = [(1 << 20) // math.isqrt(standing ** slope) + 1 for standing in range(1, number_of + 1)]
    largest = limit if full else min(limit, max(-(-total // number_of), total * weights[0] // sum(weights)))
    least = 1 if total - largest >= number_of - 1 else 0
    holding, surplus = [largest] + [least] * (number_of - 1), total - largest - least * (number_of - 1)
    while surplus > 0:
        movable = [i for i in range(1, number_of) if holding[i] < largest] or [i for i in range(1, number_of) if holding[i] < limit]
        mass, budget = sum([weights[i] for i in movable]), surplus
        for i in movable:
            extra = min(limit - holding[i], max(1, budget * weights[i] // mass), surplus)
            holding[i] = holding[i] + extra
            surplus = surplus - extra
    return np.array(holding)


def bell_draw(rng, dims, scale, reach, split=(), kind=jnp.bfloat16):
    values = scale * jax.random.normal(rng, dims, jnp.float32)
    if split:
        values = values * steps_of(rng, dims, split, -0.22, 0.18)
    return jnp.clip(values, -reach, reach).astype(kind)


def setup_inputs(seed: int = 0) -> dict:
    arg_keys = jax.random.split(jax.random.key(seed), 7)
    object_tiles = bell_draw(arg_keys[0], (SLICES, 2, N_OBJ * TILE, TILE), 0.7, 4.0, ((2, 16),))
    probe_modes = bell_draw(arg_keys[1], (MODES, 2, PX, PX), 1.0, 6.0, (), jnp.float32)
    phase_map = jnp.clip(jax.random.uniform(arg_keys[2], (PX, PX), jnp.float32, -3.140625, 3.140625), -3.140625, 3.140625)
    amplitudes = jnp.clip(0.5 + 2.5 * jax.random.uniform(arg_keys[3], (POSITIONS, PX, PX), jnp.float32) ** steps_of(arg_keys[3], (POSITIONS, PX, PX), ((0, 128),), -0.2, 0.2), 0.5, 3.0)
    offsets = plant(jax.random.randint(arg_keys[4], (POSITIONS, 2), 0, TILE - PX + 1), jax.random.fold_in(arg_keys[4], 1), 0, TILE - PX).astype(jnp.int32)
    owners_keys = jax.random.split(jax.random.fold_in(arg_keys[5], 1), POSITIONS // POS_DEV)
    owners_turns = jax.random.permutation(jax.random.fold_in(arg_keys[5], 3), POSITIONS // POS_DEV)
    owners = jax.vmap(lambda own, number: deal_out(jax.random.fold_in(arg_keys[5], 2), own, number, POS_DEV, N_OBJ, 1, CAP, 2))(owners_keys, owners_turns).reshape((POSITIONS, 1))
    return {"object_tiles": object_tiles, "probe_modes": probe_modes, "phase_map": phase_map, "amplitudes": amplitudes, "offsets": offsets, "owners": owners}


def forward_two(field):
    return jnp.fft.fft2(field, norm='ortho')

def inverse_two(field):
    return jnp.fft.ifft2(field, norm='ortho')

def position_terms(layers, measured, probe_field, kernel):
    values = layers.astype(jnp.float32)
    layer_one = lax.complex(values[0, 0], values[0, 1])
    layer_two = lax.complex(values[1, 0], values[1, 1])
    entering = probe_field * layer_one
    spread = inverse_two(kernel * forward_two(entering))
    far_field = forward_two(spread * layer_two)
    intensity = lax.optimization_barrier(jnp.sum(jnp.real(far_field) * jnp.real(far_field) + jnp.imag(far_field) * jnp.imag(far_field), axis=0))
    factor = 1.0 - measured / jnp.sqrt(jnp.maximum(intensity, 1.0))
    back_two = inverse_two(far_field * factor)
    grad_two = lax.optimization_barrier(jnp.sum(jnp.conj(spread) * back_two, axis=0))
    back_one = inverse_two(jnp.conj(kernel) * forward_two(jnp.conj(layer_two) * back_two))
    grad_one = lax.optimization_barrier(jnp.sum(jnp.conj(probe_field) * back_one, axis=0))
    grad_probe = jnp.conj(layer_one) * back_one
    patch_grad = jnp.stack([jnp.stack([jnp.real(grad_one), jnp.imag(grad_one)]), jnp.stack([jnp.real(grad_two), jnp.imag(grad_two)])]).astype(jnp.bfloat16)
    probe_grad = jnp.stack([jnp.real(grad_probe), jnp.imag(grad_probe)], axis=1)
    return (patch_grad, probe_grad)

def reference(object_tiles, probe_modes, phase_map, amplitudes, offsets, owners):
    kernel = lax.complex(jnp.cos(phase_map), jnp.sin(phase_map))
    probe_field = lax.complex(probe_modes[:, 0], probe_modes[:, 1])
    tile_stack = object_tiles.reshape(SLICES, 2, N_OBJ, TILE, TILE)

    def advance(carried, inputs):
        gradients, probe_total = carried
        measured, corner, tile_id = inputs
        anchor = jnp.zeros((), jnp.int32)
        location = (anchor, anchor, tile_id.astype(jnp.int32), corner[0].astype(jnp.int32), corner[1].astype(jnp.int32))
        window = lax.dynamic_slice(tile_stack, location, (SLICES, 2, 1, PX, PX))[:, :, 0]
        patch_grad, probe_grad = position_terms(window, measured, probe_field, kernel)
        current = lax.dynamic_slice(gradients, location, (SLICES, 2, 1, PX, PX))
        gradients = lax.dynamic_update_slice(gradients, current + patch_grad.astype(jnp.float32)[:, :, None], location)
        return ((gradients, probe_total + probe_grad), None)
    initial = (jnp.zeros((SLICES, 2, N_OBJ, TILE, TILE), jnp.float32), jnp.zeros((MODES, 2, PX, PX), jnp.float32))
    (gradients, probe_total), _ = lax.scan(advance, initial, (amplitudes, offsets, owners[:, 0]))
    return (gradients.reshape(SLICES, 2, N_OBJ * TILE, TILE), probe_total)
```

```python
import math

import jax
import jax.numpy as jnp
from jax import lax
from jax.sharding import PartitionSpec as P

highest = lax.Precision.HIGHEST


def dft_tables(length):
    counter = jnp.arange(length, dtype=jnp.int32)
    product = counter[:, None] * counter[None, :] % length
    angles = product.astype(jnp.float32) * (2.0 * math.pi / length)
    scaling = 1.0 / math.sqrt(length)
    return (jnp.cos(angles) * scaling, jnp.sin(angles) * scaling)


def right_apply(real_part, imag_part, tables, inverse):
    cosine, sines = tables
    real_cos = jnp.einsum("...ij,jk->...ik", real_part, cosine, precision=highest)
    real_sin = jnp.einsum("...ij,jk->...ik", real_part, sines, precision=highest)
    imag_cos = jnp.einsum("...ij,jk->...ik", imag_part, cosine, precision=highest)
    imag_sin = jnp.einsum("...ij,jk->...ik", imag_part, sines, precision=highest)
    if inverse:
        return (real_cos - imag_sin, imag_cos + real_sin)
    return (real_cos + imag_sin, imag_cos - real_sin)


def left_apply(real_part, imag_part, tables, inverse):
    cosine, sines = tables
    real_cos = jnp.einsum("ij,...jk->...ik", cosine, real_part, precision=highest)
    real_sin = jnp.einsum("ij,...jk->...ik", sines, real_part, precision=highest)
    imag_cos = jnp.einsum("ij,...jk->...ik", cosine, imag_part, precision=highest)
    imag_sin = jnp.einsum("ij,...jk->...ik", sines, imag_part, precision=highest)
    if inverse:
        return (real_cos - imag_sin, imag_cos + real_sin)
    return (real_cos + imag_sin, imag_cos - real_sin)


def transform(real_part, imag_part, tables, inverse):
    half_re, half_im = right_apply(real_part, imag_part, tables, inverse)
    return left_apply(half_re, half_im, tables, inverse)


def complex_mul(left_re, left_im, right_re, right_im):
    return (left_re * right_re - left_im * right_im, left_re * right_im + left_im * right_re)


def position_terms(layers, measured, weights, probe_modes, kernel, tables):
    values = layers.astype(jnp.float32)
    one_re = values[:, 0, 0][:, None]
    one_im = values[:, 0, 1][:, None]
    two_re = values[:, 1, 0][:, None]
    two_im = values[:, 1, 1][:, None]
    probe_re = probe_modes[:, 0][None]
    probe_im = probe_modes[:, 1][None]
    kern_re, kern_im = kernel
    enter_re, enter_im = complex_mul(probe_re, probe_im, one_re, one_im)
    freq_re, freq_im = transform(enter_re, enter_im, tables, False)
    freq_re, freq_im = complex_mul(freq_re, freq_im, kern_re, kern_im)
    spread_re, spread_im = transform(freq_re, freq_im, tables, True)
    leave_re, leave_im = complex_mul(spread_re, spread_im, two_re, two_im)
    far_re, far_im = transform(leave_re, leave_im, tables, False)
    intensity = jnp.sum(far_re * far_re + far_im * far_im, axis=1, keepdims=True)
    factor = 1.0 - measured[:, None] / jnp.sqrt(jnp.maximum(intensity, 1.0))
    back_re, back_im = transform(far_re * factor, far_im * factor, tables, True)
    gtwo_re, gtwo_im = complex_mul(spread_re, -spread_im, back_re, back_im)
    bspread_re, bspread_im = complex_mul(two_re, -two_im, back_re, back_im)
    freq_re, freq_im = transform(bspread_re, bspread_im, tables, False)
    freq_re, freq_im = complex_mul(freq_re, freq_im, kern_re, -kern_im)
    bone_re, bone_im = transform(freq_re, freq_im, tables, True)
    gone_re, gone_im = complex_mul(probe_re, -probe_im, bone_re, bone_im)
    gprobe_re, gprobe_im = complex_mul(one_re, -one_im, bone_re, bone_im)
    slot_weight = weights.astype(jnp.float32)
    patch_weight = slot_weight[:, None, None, None, None]
    mode_weight = slot_weight[:, None, None, None]
    grad_one = jnp.stack([jnp.sum(gone_re, axis=1), jnp.sum(gone_im, axis=1)], axis=1)
    grad_two = jnp.stack([jnp.sum(gtwo_re, axis=1), jnp.sum(gtwo_im, axis=1)], axis=1)
    patch_grad = (jnp.stack([grad_one, grad_two], axis=1) * patch_weight).astype(jnp.bfloat16)
    probe_grad = jnp.stack(
        [jnp.sum(gprobe_re * mode_weight, axis=0), jnp.sum(gprobe_im * mode_weight, axis=0)], axis=1
    )
    return (patch_grad, probe_grad)


def run_slots(windows, measured, weights, probe_modes, kernel, tables):
    slot_count = windows.shape[0]
    group_size = math.gcd(slot_count, 4)
    rounds = slot_count // group_size
    grouped = (
        windows.reshape((rounds, group_size) + windows.shape[1:]),
        measured.reshape((rounds, group_size) + measured.shape[1:]),
        weights.reshape(rounds, group_size),
    )

    def one_group(members):
        group_windows, group_measured, group_weights = members

        def active(_):
            return position_terms(
                group_windows, group_measured, group_weights, probe_modes, kernel, tables
            )

        def nothing(_):
            return (
                jnp.zeros(group_windows.shape, jnp.bfloat16),
                jnp.zeros(probe_modes.shape, jnp.float32),
            )

        return lax.cond(jnp.any(group_weights > 0), active, nothing, 0)

    gradients, probe_parts = lax.map(one_group, grouped)
    return (gradients.reshape(windows.shape), jnp.sum(probe_parts, axis=0))


def selectors(corners, width, extent, valid):
    position = jnp.arange(width, dtype=jnp.int32)
    cells = jnp.arange(extent, dtype=jnp.int32)
    rows = (cells[None, None, :] == corners[:, 0, None, None] + position[None, :, None]) & (
        valid[:, None, None] > 0
    )
    cols = cells[None, None, :] == corners[:, 1, None, None] + position[None, :, None]
    return rows.astype(jnp.bfloat16), cols.astype(jnp.bfloat16)


def accumulate(gradients, corners, valid, local_tiles):
    slots, slices, parts, width, _ = gradients.shape
    extent = local_tiles.shape[-1]
    rows, cols = selectors(corners, width, extent, valid)
    spread_cols = jnp.einsum(
        "iskab,ibc->iskac", gradients, cols, preferred_element_type=jnp.float32
    ).astype(jnp.bfloat16)
    return jnp.einsum(
        "iar,iskac->skrc", rows, spread_cols, preferred_element_type=jnp.float32
    )


def cut_windows(local_tiles, corners, width):
    extent = local_tiles.shape[-1]
    rows, cols = selectors(corners, width, extent, jnp.ones(corners.shape[:1], jnp.int32))
    picked_rows = jnp.einsum(
        "iar,skrc->iskac", rows, local_tiles, preferred_element_type=jnp.float32
    ).astype(jnp.bfloat16)
    return jnp.einsum(
        "iskac,ibc->iskab", picked_rows, cols, preferred_element_type=jnp.float32
    ).astype(jnp.bfloat16)


def on_device(object_tiles, probe_modes, phase_map, amplitudes, offsets, owners):
    tile_count = lax.axis_size("obj")
    position_count = amplitudes.shape[0]
    width = amplitudes.shape[1]
    capacity = max(2, 2 * position_count // tile_count)
    tables = dft_tables(width)
    kernel = (jnp.cos(phase_map), jnp.sin(phase_map))
    owner_ids = owners[:, 0]
    hits = (owner_ids[:, None] == jnp.arange(tile_count, dtype=jnp.int32)[None, :]).astype(
        jnp.int32
    )
    ranks = jnp.sum((jnp.cumsum(hits, axis=0) - 1) * hits, axis=1)
    destination = owner_ids * capacity + ranks
    buffer_rows = tile_count * capacity
    valid_send = jnp.zeros((buffer_rows,), jnp.int32).at[destination].set(1)
    corner_send = jnp.zeros((buffer_rows, 2), jnp.int32).at[destination].set(offsets)
    recv_corners, recv_valid = (
        lax.all_to_all(corner_send, "obj", split_axis=0, concat_axis=0, tiled=True),
        lax.all_to_all(valid_send, "obj", split_axis=0, concat_axis=0, tiled=True),
    )
    windows = cut_windows(object_tiles, recv_corners, width)
    arrived = lax.all_to_all(windows, "obj", split_axis=0, concat_axis=0, tiled=True)
    gradients, probe_part = run_slots(
        arrived[destination],
        amplitudes,
        jnp.ones((position_count,), jnp.int32),
        probe_modes,
        kernel,
        tables,
    )
    grad_buffer = jnp.zeros(arrived.shape, jnp.bfloat16).at[destination].set(gradients)
    returned = lax.all_to_all(grad_buffer, "obj", split_axis=0, concat_axis=0, tiled=True)
    running = accumulate(returned, recv_corners, recv_valid, object_tiles)
    tile_total = lax.psum(running, "scan")
    probe_total = lax.psum(probe_part, ("obj", "scan"))
    return (tile_total, probe_total)


def solution(mesh):
    placed = (
        P(None, None, "obj", None),
        P(),
        P(),
        P(("obj", "scan"), None, None),
        P(("obj", "scan"), None),
        P(("obj", "scan"), None),
    )
    return jax.shard_map(
        on_device,
        mesh=mesh,
        in_specs=placed,
        out_specs=(P(None, None, "obj", None), P()),
        check_vma=False,
    )
```

```python
import math

import jax
import jax.numpy as jnp
from jax import lax
from jax.sharding import PartitionSpec as P

highest = lax.Precision.HIGHEST


def dft_tables(length):
    counter = jnp.arange(length, dtype=jnp.int32)
    product = counter[:, None] * counter[None, :] % length
    angles = product.astype(jnp.float32) * (2.0 * math.pi / length)
    scaling = 1.0 / math.sqrt(length)
    return (jnp.cos(angles) * scaling, jnp.sin(angles) * scaling)


def right_apply(real_part, imag_part, tables, inverse):
    cosine, sines = tables
    real_cos = jnp.einsum("...ij,jk->...ik", real_part, cosine, precision=highest)
    real_sin = jnp.einsum("...ij,jk->...ik", real_part, sines, precision=highest)
    imag_cos = jnp.einsum("...ij,jk->...ik", imag_part, cosine, precision=highest)
    imag_sin = jnp.einsum("...ij,jk->...ik", imag_part, sines, precision=highest)
    if inverse:
        return (real_cos - imag_sin, imag_cos + real_sin)
    return (real_cos + imag_sin, imag_cos - real_sin)


def left_apply(real_part, imag_part, tables, inverse):
    cosine, sines = tables
    real_cos = jnp.einsum("ij,...jk->...ik", cosine, real_part, precision=highest)
    real_sin = jnp.einsum("ij,...jk->...ik", sines, real_part, precision=highest)
    imag_cos = jnp.einsum("ij,...jk->...ik", cosine, imag_part, precision=highest)
    imag_sin = jnp.einsum("ij,...jk->...ik", sines, imag_part, precision=highest)
    if inverse:
        return (real_cos - imag_sin, imag_cos + real_sin)
    return (real_cos + imag_sin, imag_cos - real_sin)


def transform(real_part, imag_part, tables, inverse):
    half_re, half_im = right_apply(real_part, imag_part, tables, inverse)
    return left_apply(half_re, half_im, tables, inverse)


def complex_mul(left_re, left_im, right_re, right_im):
    return (left_re * right_re - left_im * right_im, left_re * right_im + left_im * right_re)


def position_terms(layers, measured, weights, probe_modes, kernel, tables):
    values = layers.astype(jnp.float32)
    one_re = values[:, 0, 0][:, None]
    one_im = values[:, 0, 1][:, None]
    two_re = values[:, 1, 0][:, None]
    two_im = values[:, 1, 1][:, None]
    probe_re = probe_modes[:, 0][None]
    probe_im = probe_modes[:, 1][None]
    kern_re, kern_im = kernel
    enter_re, enter_im = complex_mul(probe_re, probe_im, one_re, one_im)
    freq_re, freq_im = transform(enter_re, enter_im, tables, False)
    freq_re, freq_im = complex_mul(freq_re, freq_im, kern_re, kern_im)
    spread_re, spread_im = transform(freq_re, freq_im, tables, True)
    leave_re, leave_im = complex_mul(spread_re, spread_im, two_re, two_im)
    far_re, far_im = transform(leave_re, leave_im, tables, False)
    intensity = jnp.sum(far_re * far_re + far_im * far_im, axis=1, keepdims=True)
    factor = 1.0 - measured[:, None] / jnp.sqrt(jnp.maximum(intensity, 1.0))
    back_re, back_im = transform(far_re * factor, far_im * factor, tables, True)
    gtwo_re, gtwo_im = complex_mul(spread_re, -spread_im, back_re, back_im)
    bspread_re, bspread_im = complex_mul(two_re, -two_im, back_re, back_im)
    freq_re, freq_im = transform(bspread_re, bspread_im, tables, False)
    freq_re, freq_im = complex_mul(freq_re, freq_im, kern_re, -kern_im)
    bone_re, bone_im = transform(freq_re, freq_im, tables, True)
    gone_re, gone_im = complex_mul(probe_re, -probe_im, bone_re, bone_im)
    gprobe_re, gprobe_im = complex_mul(one_re, -one_im, bone_re, bone_im)
    slot_weight = weights.astype(jnp.float32)
    patch_weight = slot_weight[:, None, None, None, None]
    mode_weight = slot_weight[:, None, None, None]
    grad_one = jnp.stack([jnp.sum(gone_re, axis=1), jnp.sum(gone_im, axis=1)], axis=1)
    grad_two = jnp.stack([jnp.sum(gtwo_re, axis=1), jnp.sum(gtwo_im, axis=1)], axis=1)
    patch_grad = (jnp.stack([grad_one, grad_two], axis=1) * patch_weight).astype(jnp.bfloat16)
    probe_grad = jnp.stack(
        [jnp.sum(gprobe_re * mode_weight, axis=0), jnp.sum(gprobe_im * mode_weight, axis=0)], axis=1
    )
    return (patch_grad, probe_grad)


def run_slots(windows, measured, weights, probe_modes, kernel, tables):
    slot_count = windows.shape[0]
    group_size = math.gcd(slot_count, 4)
    rounds = slot_count // group_size
    grouped = (
        windows.reshape((rounds, group_size) + windows.shape[1:]),
        measured.reshape((rounds, group_size) + measured.shape[1:]),
        weights.reshape(rounds, group_size),
    )

    def one_group(members):
        group_windows, group_measured, group_weights = members

        def active(_):
            return position_terms(
                group_windows, group_measured, group_weights, probe_modes, kernel, tables
            )

        def nothing(_):
            return (
                jnp.zeros(group_windows.shape, jnp.bfloat16),
                jnp.zeros(probe_modes.shape, jnp.float32),
            )

        return lax.cond(jnp.any(group_weights > 0), active, nothing, 0)

    gradients, probe_parts = lax.map(one_group, grouped)
    return (gradients.reshape(windows.shape), jnp.sum(probe_parts, axis=0))


def selectors(corners, width, extent, valid):
    position = jnp.arange(width, dtype=jnp.int32)
    cells = jnp.arange(extent, dtype=jnp.int32)
    rows = (cells[None, None, :] == corners[:, 0, None, None] + position[None, :, None]) & (
        valid[:, None, None] > 0
    )
    cols = cells[None, None, :] == corners[:, 1, None, None] + position[None, :, None]
    return rows.astype(jnp.bfloat16), cols.astype(jnp.bfloat16)


def accumulate(gradients, corners, valid, local_tiles):
    slots, slices, parts, width, _ = gradients.shape
    extent = local_tiles.shape[-1]
    rows, cols = selectors(corners, width, extent, valid)
    spread_cols = jnp.einsum(
        "iskab,ibc->iskac", gradients, cols, preferred_element_type=jnp.float32
    ).astype(jnp.bfloat16)
    return jnp.einsum(
        "iar,iskac->skrc", rows, spread_cols, preferred_element_type=jnp.float32
    )


def cut_windows(local_tiles, corners, width):
    extent = local_tiles.shape[-1]
    rows, cols = selectors(corners, width, extent, jnp.ones(corners.shape[:1], jnp.int32))
    picked_rows = jnp.einsum(
        "iar,skrc->iskac", rows, local_tiles, preferred_element_type=jnp.float32
    ).astype(jnp.bfloat16)
    return jnp.einsum(
        "iskac,ibc->iskab", picked_rows, cols, preferred_element_type=jnp.float32
    ).astype(jnp.bfloat16)


def on_device(object_tiles, probe_modes, phase_map, amplitudes, offsets, owners):
    tile_count = lax.axis_size("obj")
    position_count = amplitudes.shape[0]
    width = amplitudes.shape[1]
    capacity = max(2, 2 * position_count // tile_count)
    tables = dft_tables(width)
    kernel = (jnp.cos(phase_map), jnp.sin(phase_map))
    owner_ids = owners[:, 0]
    hits = (owner_ids[:, None] == jnp.arange(tile_count, dtype=jnp.int32)[None, :]).astype(
        jnp.int32
    )
    ranks = jnp.sum((jnp.cumsum(hits, axis=0) - 1) * hits, axis=1)
    destination = owner_ids * capacity + ranks
    buffer_rows = tile_count * capacity
    marked = jnp.concatenate([offsets, jnp.ones((position_count, 1), jnp.int32)], axis=1)
    request_send = jnp.zeros((buffer_rows, 3), jnp.int32).at[destination].set(marked)
    requests = lax.all_to_all(request_send, "obj", split_axis=0, concat_axis=0, tiled=True)
    recv_corners, recv_valid = requests[:, :2], requests[:, 2]
    windows = cut_windows(object_tiles, recv_corners, width)
    arrived = lax.all_to_all(windows, "obj", split_axis=0, concat_axis=0, tiled=True)
    gradients, probe_part = run_slots(
        arrived[destination],
        amplitudes,
        jnp.ones((position_count,), jnp.int32),
        probe_modes,
        kernel,
        tables,
    )
    grad_buffer = jnp.zeros(arrived.shape, jnp.bfloat16).at[destination].set(gradients)
    returned = lax.all_to_all(grad_buffer, "obj", split_axis=0, concat_axis=0, tiled=True)
    running = accumulate(returned, recv_corners, recv_valid, object_tiles)
    probe_obj = lax.psum(probe_part, "obj")
    joined = jnp.concatenate([running.reshape(-1), probe_obj.reshape(-1)])
    joined = lax.psum(joined, "scan")
    tile_total = joined[: running.size].reshape(running.shape)
    probe_total = joined[running.size :].reshape(probe_part.shape)
    return (tile_total, probe_total)


def solution(mesh):
    placed = (
        P(None, None, "obj", None),
        P(),
        P(),
        P(("obj", "scan"), None, None),
        P(("obj", "scan"), None),
        P(("obj", "scan"), None),
    )
    return jax.shard_map(
        on_device,
        mesh=mesh,
        in_specs=placed,
        out_specs=(P(None, None, "obj", None), P()),
        check_vma=False,
    )
```

```python
import math

import jax
import numpy as np
import jax.numpy as jnp
from jax import lax
from jax.sharding import PartitionSpec as P
from jax.experimental import pallas as pl
from jax.experimental.pallas import tpu as pltpu

highest = lax.Precision.HIGHEST


def dft_tables(length):
    counter = jnp.arange(length, dtype=jnp.int32)
    product = counter[:, None] * counter[None, :] % length
    angles = product.astype(jnp.float32) * (2.0 * math.pi / length)
    scaling = 1.0 / math.sqrt(length)
    return (jnp.cos(angles) * scaling, jnp.sin(angles) * scaling)


def right_apply(real_part, imag_part, tables, inverse):
    cosine, sines = tables
    real_cos = jnp.einsum("...ij,jk->...ik", real_part, cosine, precision=highest)
    real_sin = jnp.einsum("...ij,jk->...ik", real_part, sines, precision=highest)
    imag_cos = jnp.einsum("...ij,jk->...ik", imag_part, cosine, precision=highest)
    imag_sin = jnp.einsum("...ij,jk->...ik", imag_part, sines, precision=highest)
    if inverse:
        return (real_cos - imag_sin, imag_cos + real_sin)
    return (real_cos + imag_sin, imag_cos - real_sin)


def left_apply(real_part, imag_part, tables, inverse):
    cosine, sines = tables
    real_cos = jnp.einsum("ij,...jk->...ik", cosine, real_part, precision=highest)
    real_sin = jnp.einsum("ij,...jk->...ik", sines, real_part, precision=highest)
    imag_cos = jnp.einsum("ij,...jk->...ik", cosine, imag_part, precision=highest)
    imag_sin = jnp.einsum("ij,...jk->...ik", sines, imag_part, precision=highest)
    if inverse:
        return (real_cos - imag_sin, imag_cos + real_sin)
    return (real_cos + imag_sin, imag_cos - real_sin)


def transform(real_part, imag_part, tables, inverse):
    half_re, half_im = right_apply(real_part, imag_part, tables, inverse)
    return left_apply(half_re, half_im, tables, inverse)


def complex_mul(left_re, left_im, right_re, right_im):
    return (left_re * right_re - left_im * right_im, left_re * right_im + left_im * right_re)


def position_terms(layers, measured, weights, probe_modes, kernel, tables):
    values = layers.astype(jnp.float32)
    one_re = values[:, 0, 0][:, None]
    one_im = values[:, 0, 1][:, None]
    two_re = values[:, 1, 0][:, None]
    two_im = values[:, 1, 1][:, None]
    probe_re = probe_modes[:, 0][None]
    probe_im = probe_modes[:, 1][None]
    kern_re, kern_im = kernel
    enter_re, enter_im = complex_mul(probe_re, probe_im, one_re, one_im)
    freq_re, freq_im = transform(enter_re, enter_im, tables, False)
    freq_re, freq_im = complex_mul(freq_re, freq_im, kern_re, kern_im)
    spread_re, spread_im = transform(freq_re, freq_im, tables, True)
    leave_re, leave_im = complex_mul(spread_re, spread_im, two_re, two_im)
    far_re, far_im = transform(leave_re, leave_im, tables, False)
    intensity = jnp.sum(far_re * far_re + far_im * far_im, axis=1, keepdims=True)
    factor = 1.0 - measured[:, None] / jnp.sqrt(jnp.maximum(intensity, 1.0))
    back_re, back_im = transform(far_re * factor, far_im * factor, tables, True)
    gtwo_re, gtwo_im = complex_mul(spread_re, -spread_im, back_re, back_im)
    bspread_re, bspread_im = complex_mul(two_re, -two_im, back_re, back_im)
    freq_re, freq_im = transform(bspread_re, bspread_im, tables, False)
    freq_re, freq_im = complex_mul(freq_re, freq_im, kern_re, -kern_im)
    bone_re, bone_im = transform(freq_re, freq_im, tables, True)
    gone_re, gone_im = complex_mul(probe_re, -probe_im, bone_re, bone_im)
    gprobe_re, gprobe_im = complex_mul(one_re, -one_im, bone_re, bone_im)
    slot_weight = weights.astype(jnp.float32)
    patch_weight = slot_weight[:, None, None, None, None]
    mode_weight = slot_weight[:, None, None, None]
    grad_one = jnp.stack([jnp.sum(gone_re, axis=1), jnp.sum(gone_im, axis=1)], axis=1)
    grad_two = jnp.stack([jnp.sum(gtwo_re, axis=1), jnp.sum(gtwo_im, axis=1)], axis=1)
    patch_grad = (jnp.stack([grad_one, grad_two], axis=1) * patch_weight).astype(jnp.bfloat16)
    probe_grad = jnp.stack(
        [jnp.sum(gprobe_re * mode_weight, axis=0), jnp.sum(gprobe_im * mode_weight, axis=0)], axis=1
    )
    return (patch_grad, probe_grad)


def run_slots(windows, measured, weights, probe_modes, kernel, tables):
    slot_count = windows.shape[0]
    group_size = math.gcd(slot_count, 4)
    rounds = slot_count // group_size
    grouped = (
        windows.reshape((rounds, group_size) + windows.shape[1:]),
        measured.reshape((rounds, group_size) + measured.shape[1:]),
        weights.reshape(rounds, group_size),
    )

    def one_group(members):
        group_windows, group_measured, group_weights = members

        def active(_):
            return position_terms(
                group_windows, group_measured, group_weights, probe_modes, kernel, tables
            )

        def nothing(_):
            return (
                jnp.zeros(group_windows.shape, jnp.bfloat16),
                jnp.zeros(probe_modes.shape, jnp.float32),
            )

        return lax.cond(jnp.any(group_weights > 0), active, nothing, 0)

    gradients, probe_parts = lax.map(one_group, grouped)
    return (gradients.reshape(windows.shape), jnp.sum(probe_parts, axis=0))


def split_bf16(values):
    high = values.astype(jnp.bfloat16)
    low = (values - high.astype(jnp.float32)).astype(jnp.bfloat16)
    return high, low


def stacked_tables(width):
    counter = np.arange(width)
    angles = (counter[:, None] * counter[None, :] % width) * (2.0 * np.pi / width)
    cosine = np.cos(angles) / np.sqrt(width)
    sines = np.sin(angles) / np.sqrt(width)
    forward = np.block([[cosine, -sines], [sines, cosine]])
    inverse = np.block([[cosine, sines], [-sines, cosine]])
    both = np.stack([forward, inverse])
    high = both.astype(jnp.bfloat16)
    low = (both - high.astype(np.float64)).astype(jnp.bfloat16)
    return jnp.asarray(np.stack([high, low], axis=1))


def split_dot(left, right, left_split, right_split):
    left_high, left_low = left_split(left)
    right_high, right_low = right_split(right)
    total = jnp.dot(left_high, right_high, preferred_element_type=jnp.float32)
    total = total + jnp.dot(left_low, right_high, preferred_element_type=jnp.float32)
    return total + jnp.dot(left_high, right_low, preferred_element_type=jnp.float32)


def position_kernel(window_ref, measured_ref, probe_ref, phase_ref, table_ref, patch_ref, probe_out_ref,
                    spread_ref, far_ref):
    width = measured_ref.shape[-1]
    modes = probe_ref.shape[0]

    @pl.when(pl.program_id(0) == 0)
    def _():
        probe_out_ref[...] = jnp.zeros(probe_out_ref.shape, jnp.float32)

    def table(index):
        return lambda _: (table_ref[index, 0], table_ref[index, 1])

    def transform(real_part, imag_part, inverse):
        right_index = 1 if inverse else 0
        joined = jnp.concatenate([real_part, imag_part], axis=1)
        half = split_dot(joined, None, split_bf16, table(right_index))
        stacked = jnp.concatenate([half[:, :width], half[:, width:]], axis=0)
        full = split_dot(None, stacked, table(1 - right_index), split_bf16)
        return full[:width], full[width:]

    one_re = window_ref[0, 0, 0].astype(jnp.float32)
    one_im = window_ref[0, 0, 1].astype(jnp.float32)
    two_re = window_ref[0, 1, 0].astype(jnp.float32)
    two_im = window_ref[0, 1, 1].astype(jnp.float32)
    kern_re = phase_ref[0]
    kern_im = phase_ref[1]

    def forward_mode(mode, intensity):
        probe_re = probe_ref[mode, 0]
        probe_im = probe_ref[mode, 1]
        enter_re, enter_im = complex_mul(probe_re, probe_im, one_re, one_im)
        freq_re, freq_im = transform(enter_re, enter_im, False)
        freq_re, freq_im = complex_mul(freq_re, freq_im, kern_re, kern_im)
        spread_re, spread_im = transform(freq_re, freq_im, True)
        leave_re, leave_im = complex_mul(spread_re, spread_im, two_re, two_im)
        far_re, far_im = transform(leave_re, leave_im, False)
        spread_ref[mode, 0] = spread_re
        spread_ref[mode, 1] = spread_im
        far_ref[mode, 0] = far_re
        far_ref[mode, 1] = far_im
        return intensity + far_re * far_re + far_im * far_im

    intensity = lax.fori_loop(0, modes, forward_mode, jnp.zeros((width, width), jnp.float32))
    factor = 1.0 - measured_ref[0] / jnp.sqrt(jnp.maximum(intensity, 1.0))

    def backward_mode(mode, carried):
        gone_re, gone_im, gtwo_re, gtwo_im = carried
        probe_re = probe_ref[mode, 0]
        probe_im = probe_ref[mode, 1]
        spread_re = spread_ref[mode, 0]
        spread_im = spread_ref[mode, 1]
        back_re, back_im = transform(far_ref[mode, 0] * factor, far_ref[mode, 1] * factor, True)
        add_re, add_im = complex_mul(spread_re, -spread_im, back_re, back_im)
        bspread_re, bspread_im = complex_mul(two_re, -two_im, back_re, back_im)
        freq_re, freq_im = transform(bspread_re, bspread_im, False)
        freq_re, freq_im = complex_mul(freq_re, freq_im, kern_re, -kern_im)
        bone_re, bone_im = transform(freq_re, freq_im, True)
        one_add_re, one_add_im = complex_mul(probe_re, -probe_im, bone_re, bone_im)
        term_re, term_im = complex_mul(one_re, -one_im, bone_re, bone_im)
        probe_out_ref[mode, 0] = probe_out_ref[mode, 0] + term_re
        probe_out_ref[mode, 1] = probe_out_ref[mode, 1] + term_im
        return (gone_re + one_add_re, gone_im + one_add_im, gtwo_re + add_re, gtwo_im + add_im)

    zeros = jnp.zeros((width, width), jnp.float32)
    gone_re, gone_im, gtwo_re, gtwo_im = lax.fori_loop(
        0, modes, backward_mode, (zeros, zeros, zeros, zeros)
    )
    patch_ref[0, 0, 0] = gone_re.astype(patch_ref.dtype)
    patch_ref[0, 0, 1] = gone_im.astype(patch_ref.dtype)
    patch_ref[0, 1, 0] = gtwo_re.astype(patch_ref.dtype)
    patch_ref[0, 1, 1] = gtwo_im.astype(patch_ref.dtype)


def run_positions(windows, measured, probe_modes, phase_map):
    count, width = measured.shape[0], measured.shape[-1]
    modes = probe_modes.shape[0]
    tables = stacked_tables(width)
    phases = jnp.stack([jnp.cos(phase_map), jnp.sin(phase_map)])
    flops = count * modes * 6 * 2 * 3 * 2 * width * (2 * width) * (2 * width)
    return pl.pallas_call(
        position_kernel,
        grid=(count,),
        in_specs=[
            pl.BlockSpec((1,) + windows.shape[1:], lambda p: (p, 0, 0, 0, 0)),
            pl.BlockSpec((1, width, width), lambda p: (p, 0, 0)),
            pl.BlockSpec(probe_modes.shape, lambda p: (0, 0, 0, 0)),
            pl.BlockSpec(phases.shape, lambda p: (0, 0, 0)),
            pl.BlockSpec(tables.shape, lambda p: (0, 0, 0, 0)),
        ],
        out_specs=[
            pl.BlockSpec((1,) + windows.shape[1:], lambda p: (p, 0, 0, 0, 0)),
            pl.BlockSpec(probe_modes.shape, lambda p: (0, 0, 0, 0)),
        ],
        out_shape=[
            jax.ShapeDtypeStruct(windows.shape, jnp.bfloat16),
            jax.ShapeDtypeStruct(probe_modes.shape, jnp.float32),
        ],
        scratch_shapes=[
            pltpu.VMEM((modes, 2, width, width), jnp.float32),
            pltpu.VMEM((modes, 2, width, width), jnp.float32),
        ],
        compiler_params=pltpu.CompilerParams(dimension_semantics=("arbitrary",)),
        cost_estimate=pl.CostEstimate(
            flops=flops, transcendentals=count * width * width, bytes_accessed=count * 6 * width * width * 4
        ),
    )(windows, measured, probe_modes, phases, tables)


def selectors(corners, width, extent, valid):
    position = jnp.arange(width, dtype=jnp.int32)
    cells = jnp.arange(extent, dtype=jnp.int32)
    rows = (cells[None, None, :] == corners[:, 0, None, None] + position[None, :, None]) & (
        valid[:, None, None] > 0
    )
    cols = cells[None, None, :] == corners[:, 1, None, None] + position[None, :, None]
    return rows.astype(jnp.bfloat16), cols.astype(jnp.bfloat16)


def accumulate(gradients, corners, valid, local_tiles):
    slots, slices, parts, width, _ = gradients.shape
    extent = local_tiles.shape[-1]
    rows, cols = selectors(corners, width, extent, valid)
    spread_cols = jnp.einsum(
        "iskab,ibc->iskac", gradients, cols, preferred_element_type=jnp.float32
    ).astype(jnp.bfloat16)
    return jnp.einsum(
        "iar,iskac->skrc", rows, spread_cols, preferred_element_type=jnp.float32
    )


def cut_windows(local_tiles, corners, width):
    extent = local_tiles.shape[-1]
    rows, cols = selectors(corners, width, extent, jnp.ones(corners.shape[:1], jnp.int32))
    picked_rows = jnp.einsum(
        "iar,skrc->iskac", rows, local_tiles, preferred_element_type=jnp.float32
    ).astype(jnp.bfloat16)
    return jnp.einsum(
        "iskac,ibc->iskab", picked_rows, cols, preferred_element_type=jnp.float32
    ).astype(jnp.bfloat16)


def on_device(object_tiles, probe_modes, phase_map, amplitudes, offsets, owners):
    tile_count = lax.axis_size("obj")
    position_count = amplitudes.shape[0]
    width = amplitudes.shape[1]
    capacity = max(2, 2 * position_count // tile_count)
    owner_ids = owners[:, 0]
    hits = (owner_ids[:, None] == jnp.arange(tile_count, dtype=jnp.int32)[None, :]).astype(
        jnp.int32
    )
    ranks = jnp.sum((jnp.cumsum(hits, axis=0) - 1) * hits, axis=1)
    destination = owner_ids * capacity + ranks
    buffer_rows = tile_count * capacity
    marked = jnp.concatenate([offsets, jnp.ones((position_count, 1), jnp.int32)], axis=1)
    request_send = jnp.zeros((buffer_rows, 3), jnp.int32).at[destination].set(marked)
    requests = lax.all_to_all(request_send, "obj", split_axis=0, concat_axis=0, tiled=True)
    recv_corners, recv_valid = requests[:, :2], requests[:, 2]
    windows = cut_windows(object_tiles, recv_corners, width)
    arrived = lax.all_to_all(windows, "obj", split_axis=0, concat_axis=0, tiled=True)
    gradients, probe_part = run_positions(arrived[destination], amplitudes, probe_modes, phase_map)
    grad_buffer = jnp.zeros(arrived.shape, jnp.bfloat16).at[destination].set(gradients)
    returned = lax.all_to_all(grad_buffer, "obj", split_axis=0, concat_axis=0, tiled=True)
    running = accumulate(returned, recv_corners, recv_valid, object_tiles)
    probe_obj = lax.psum(probe_part, "obj")
    joined = jnp.concatenate([running.reshape(-1), probe_obj.reshape(-1)])
    joined = lax.psum(joined, "scan")
    tile_total = joined[: running.size].reshape(running.shape)
    probe_total = joined[running.size :].reshape(probe_part.shape)
    return (tile_total, probe_total)


def solution(mesh):
    placed = (
        P(None, None, "obj", None),
        P(),
        P(),
        P(("obj", "scan"), None, None),
        P(("obj", "scan"), None),
        P(("obj", "scan"), None),
    )
    return jax.shard_map(
        on_device,
        mesh=mesh,
        in_specs=placed,
        out_specs=(P(None, None, "obj", None), P()),
        check_vma=False,
    )
```

```python
import math

import jax
import numpy as np
import jax.numpy as jnp
from jax import lax
from jax.sharding import PartitionSpec as P
from jax.experimental import pallas as pl
from jax.experimental.pallas import tpu as pltpu

highest = lax.Precision.HIGHEST


def dft_tables(length):
    counter = jnp.arange(length, dtype=jnp.int32)
    product = counter[:, None] * counter[None, :] % length
    angles = product.astype(jnp.float32) * (2.0 * math.pi / length)
    scaling = 1.0 / math.sqrt(length)
    return (jnp.cos(angles) * scaling, jnp.sin(angles) * scaling)


def right_apply(real_part, imag_part, tables, inverse):
    cosine, sines = tables
    real_cos = jnp.einsum("...ij,jk->...ik", real_part, cosine, precision=highest)
    real_sin = jnp.einsum("...ij,jk->...ik", real_part, sines, precision=highest)
    imag_cos = jnp.einsum("...ij,jk->...ik", imag_part, cosine, precision=highest)
    imag_sin = jnp.einsum("...ij,jk->...ik", imag_part, sines, precision=highest)
    if inverse:
        return (real_cos - imag_sin, imag_cos + real_sin)
    return (real_cos + imag_sin, imag_cos - real_sin)


def left_apply(real_part, imag_part, tables, inverse):
    cosine, sines = tables
    real_cos = jnp.einsum("ij,...jk->...ik", cosine, real_part, precision=highest)
    real_sin = jnp.einsum("ij,...jk->...ik", sines, real_part, precision=highest)
    imag_cos = jnp.einsum("ij,...jk->...ik", cosine, imag_part, precision=highest)
    imag_sin = jnp.einsum("ij,...jk->...ik", sines, imag_part, precision=highest)
    if inverse:
        return (real_cos - imag_sin, imag_cos + real_sin)
    return (real_cos + imag_sin, imag_cos - real_sin)


def transform(real_part, imag_part, tables, inverse):
    half_re, half_im = right_apply(real_part, imag_part, tables, inverse)
    return left_apply(half_re, half_im, tables, inverse)


def complex_mul(left_re, left_im, right_re, right_im):
    return (left_re * right_re - left_im * right_im, left_re * right_im + left_im * right_re)


def position_terms(layers, measured, weights, probe_modes, kernel, tables):
    values = layers.astype(jnp.float32)
    one_re = values[:, 0, 0][:, None]
    one_im = values[:, 0, 1][:, None]
    two_re = values[:, 1, 0][:, None]
    two_im = values[:, 1, 1][:, None]
    probe_re = probe_modes[:, 0][None]
    probe_im = probe_modes[:, 1][None]
    kern_re, kern_im = kernel
    enter_re, enter_im = complex_mul(probe_re, probe_im, one_re, one_im)
    freq_re, freq_im = transform(enter_re, enter_im, tables, False)
    freq_re, freq_im = complex_mul(freq_re, freq_im, kern_re, kern_im)
    spread_re, spread_im = transform(freq_re, freq_im, tables, True)
    leave_re, leave_im = complex_mul(spread_re, spread_im, two_re, two_im)
    far_re, far_im = transform(leave_re, leave_im, tables, False)
    intensity = jnp.sum(far_re * far_re + far_im * far_im, axis=1, keepdims=True)
    factor = 1.0 - measured[:, None] / jnp.sqrt(jnp.maximum(intensity, 1.0))
    back_re, back_im = transform(far_re * factor, far_im * factor, tables, True)
    gtwo_re, gtwo_im = complex_mul(spread_re, -spread_im, back_re, back_im)
    bspread_re, bspread_im = complex_mul(two_re, -two_im, back_re, back_im)
    freq_re, freq_im = transform(bspread_re, bspread_im, tables, False)
    freq_re, freq_im = complex_mul(freq_re, freq_im, kern_re, -kern_im)
    bone_re, bone_im = transform(freq_re, freq_im, tables, True)
    gone_re, gone_im = complex_mul(probe_re, -probe_im, bone_re, bone_im)
    gprobe_re, gprobe_im = complex_mul(one_re, -one_im, bone_re, bone_im)
    slot_weight = weights.astype(jnp.float32)
    patch_weight = slot_weight[:, None, None, None, None]
    mode_weight = slot_weight[:, None, None, None]
    grad_one = jnp.stack([jnp.sum(gone_re, axis=1), jnp.sum(gone_im, axis=1)], axis=1)
    grad_two = jnp.stack([jnp.sum(gtwo_re, axis=1), jnp.sum(gtwo_im, axis=1)], axis=1)
    patch_grad = (jnp.stack([grad_one, grad_two], axis=1) * patch_weight).astype(jnp.bfloat16)
    probe_grad = jnp.stack(
        [jnp.sum(gprobe_re * mode_weight, axis=0), jnp.sum(gprobe_im * mode_weight, axis=0)], axis=1
    )
    return (patch_grad, probe_grad)


def run_slots(windows, measured, weights, probe_modes, kernel, tables):
    slot_count = windows.shape[0]
    group_size = math.gcd(slot_count, 4)
    rounds = slot_count // group_size
    grouped = (
        windows.reshape((rounds, group_size) + windows.shape[1:]),
        measured.reshape((rounds, group_size) + measured.shape[1:]),
        weights.reshape(rounds, group_size),
    )

    def one_group(members):
        group_windows, group_measured, group_weights = members

        def active(_):
            return position_terms(
                group_windows, group_measured, group_weights, probe_modes, kernel, tables
            )

        def nothing(_):
            return (
                jnp.zeros(group_windows.shape, jnp.bfloat16),
                jnp.zeros(probe_modes.shape, jnp.float32),
            )

        return lax.cond(jnp.any(group_weights > 0), active, nothing, 0)

    gradients, probe_parts = lax.map(one_group, grouped)
    return (gradients.reshape(windows.shape), jnp.sum(probe_parts, axis=0))


def split_bf16(values):
    high = values.astype(jnp.bfloat16)
    low = (values - high.astype(jnp.float32)).astype(jnp.bfloat16)
    return high, low


def stacked_tables(width):
    counter = np.arange(width)
    angles = (counter[:, None] * counter[None, :] % width) * (2.0 * np.pi / width)
    cosine = np.cos(angles) / np.sqrt(width)
    sines = np.sin(angles) / np.sqrt(width)
    forward = np.block([[cosine, -sines], [sines, cosine]])
    inverse = np.block([[cosine, sines], [-sines, cosine]])
    both = np.stack([forward, inverse])
    high = both.astype(jnp.bfloat16)
    low = (both - high.astype(np.float64)).astype(jnp.bfloat16)
    return jnp.asarray(np.stack([high, low], axis=1))


def split_dot(left, right, left_split, right_split):
    left_high, left_low = left_split(left)
    right_high, right_low = right_split(right)
    total = jnp.dot(left_high, right_high, preferred_element_type=jnp.float32)
    total = total + jnp.dot(left_low, right_high, preferred_element_type=jnp.float32)
    return total + jnp.dot(left_high, right_low, preferred_element_type=jnp.float32)


def position_kernel(window_ref, measured_ref, probe_ref, phase_ref, table_ref, patch_ref, probe_out_ref):
    width = measured_ref.shape[-1]
    modes = probe_ref.shape[0]

    @pl.when(pl.program_id(0) == 0)
    def _():
        probe_out_ref[...] = jnp.zeros(probe_out_ref.shape, jnp.float32)

    def table(index):
        return lambda _: (table_ref[index, 0], table_ref[index, 1])

    def transform(reals, imags, inverse):
        right_index = 1 if inverse else 0
        joined = jnp.concatenate(
            [jnp.concatenate([real, imag], axis=1) for real, imag in zip(reals, imags)], axis=0
        )
        half = split_dot(joined, None, split_bf16, table(right_index))
        stacked = jnp.concatenate(
            [
                jnp.concatenate(
                    [half[m * width:(m + 1) * width, :width], half[m * width:(m + 1) * width, width:]],
                    axis=0,
                )
                for m in range(len(reals))
            ],
            axis=1,
        )
        full = split_dot(None, stacked, table(1 - right_index), split_bf16)
        return (
            [full[:width, m * width:(m + 1) * width] for m in range(len(reals))],
            [full[width:, m * width:(m + 1) * width] for m in range(len(reals))],
        )

    def each(function, *lists):
        results = [function(*members) for members in zip(*lists)]
        return [r[0] for r in results], [r[1] for r in results]

    one_re = window_ref[0, 0, 0].astype(jnp.float32)
    one_im = window_ref[0, 0, 1].astype(jnp.float32)
    two_re = window_ref[0, 1, 0].astype(jnp.float32)
    two_im = window_ref[0, 1, 1].astype(jnp.float32)
    kern_re = phase_ref[0]
    kern_im = phase_ref[1]
    probe_re = [probe_ref[m, 0] for m in range(modes)]
    probe_im = [probe_ref[m, 1] for m in range(modes)]

    enter = each(lambda a, b: complex_mul(a, b, one_re, one_im), probe_re, probe_im)
    freq = transform(*enter, False)
    freq = each(lambda a, b: complex_mul(a, b, kern_re, kern_im), *freq)
    spread_re, spread_im = transform(*freq, True)
    leave = each(lambda a, b: complex_mul(a, b, two_re, two_im), spread_re, spread_im)
    far_re, far_im = transform(*leave, False)
    intensity = far_re[0] * far_re[0] + far_im[0] * far_im[0]
    for m in range(1, modes):
        intensity = intensity + far_re[m] * far_re[m] + far_im[m] * far_im[m]
    factor = 1.0 - measured_ref[0] / jnp.sqrt(jnp.maximum(intensity, 1.0))
    back_re, back_im = transform([f * factor for f in far_re], [f * factor for f in far_im], True)
    gtwo = each(lambda a, b, c, d: complex_mul(a, -b, c, d), spread_re, spread_im, back_re, back_im)
    bspread = each(lambda a, b: complex_mul(two_re, -two_im, a, b), back_re, back_im)
    freq = transform(*bspread, False)
    freq = each(lambda a, b: complex_mul(a, b, kern_re, -kern_im), *freq)
    bone_re, bone_im = transform(*freq, True)
    gone = each(lambda a, b, c, d: complex_mul(a, -b, c, d), probe_re, probe_im, bone_re, bone_im)
    for m in range(modes):
        term_re, term_im = complex_mul(one_re, -one_im, bone_re[m], bone_im[m])
        probe_out_ref[m, 0] = probe_out_ref[m, 0] + term_re
        probe_out_ref[m, 1] = probe_out_ref[m, 1] + term_im
    patch_ref[0, 0, 0] = sum(gone[0][1:], gone[0][0]).astype(patch_ref.dtype)
    patch_ref[0, 0, 1] = sum(gone[1][1:], gone[1][0]).astype(patch_ref.dtype)
    patch_ref[0, 1, 0] = sum(gtwo[0][1:], gtwo[0][0]).astype(patch_ref.dtype)
    patch_ref[0, 1, 1] = sum(gtwo[1][1:], gtwo[1][0]).astype(patch_ref.dtype)


def run_positions(windows, measured, probe_modes, phase_map):
    count, width = measured.shape[0], measured.shape[-1]
    modes = probe_modes.shape[0]
    tables = stacked_tables(width)
    phases = jnp.stack([jnp.cos(phase_map), jnp.sin(phase_map)])
    flops = count * modes * 6 * 2 * 3 * 2 * width * (2 * width) * (2 * width)
    return pl.pallas_call(
        position_kernel,
        grid=(count,),
        in_specs=[
            pl.BlockSpec((1,) + windows.shape[1:], lambda p: (p, 0, 0, 0, 0)),
            pl.BlockSpec((1, width, width), lambda p: (p, 0, 0)),
            pl.BlockSpec(probe_modes.shape, lambda p: (0, 0, 0, 0)),
            pl.BlockSpec(phases.shape, lambda p: (0, 0, 0)),
            pl.BlockSpec(tables.shape, lambda p: (0, 0, 0, 0)),
        ],
        out_specs=[
            pl.BlockSpec((1,) + windows.shape[1:], lambda p: (p, 0, 0, 0, 0)),
            pl.BlockSpec(probe_modes.shape, lambda p: (0, 0, 0, 0)),
        ],
        out_shape=[
            jax.ShapeDtypeStruct(windows.shape, jnp.bfloat16),
            jax.ShapeDtypeStruct(probe_modes.shape, jnp.float32),
        ],
        compiler_params=pltpu.CompilerParams(dimension_semantics=("arbitrary",)),
        cost_estimate=pl.CostEstimate(
            flops=flops, transcendentals=count * width * width, bytes_accessed=count * 6 * width * width * 4
        ),
    )(windows, measured, probe_modes, phases, tables)


def selectors(corners, width, extent, valid):
    position = jnp.arange(width, dtype=jnp.int32)
    cells = jnp.arange(extent, dtype=jnp.int32)
    rows = (cells[None, None, :] == corners[:, 0, None, None] + position[None, :, None]) & (
        valid[:, None, None] > 0
    )
    cols = cells[None, None, :] == corners[:, 1, None, None] + position[None, :, None]
    return rows.astype(jnp.bfloat16), cols.astype(jnp.bfloat16)


def accumulate(gradients, corners, valid, local_tiles):
    slots, slices, parts, width, _ = gradients.shape
    extent = local_tiles.shape[-1]
    rows, cols = selectors(corners, width, extent, valid)
    spread_cols = jnp.einsum(
        "iskab,ibc->iskac", gradients, cols, preferred_element_type=jnp.float32
    ).astype(jnp.bfloat16)
    return jnp.einsum(
        "iar,iskac->skrc", rows, spread_cols, preferred_element_type=jnp.float32
    )


def cut_windows(local_tiles, corners, width):
    extent = local_tiles.shape[-1]
    rows, cols = selectors(corners, width, extent, jnp.ones(corners.shape[:1], jnp.int32))
    picked_rows = jnp.einsum(
        "iar,skrc->iskac", rows, local_tiles, preferred_element_type=jnp.float32
    ).astype(jnp.bfloat16)
    return jnp.einsum(
        "iskac,ibc->iskab", picked_rows, cols, preferred_element_type=jnp.float32
    ).astype(jnp.bfloat16)


def on_device(object_tiles, probe_modes, phase_map, amplitudes, offsets, owners):
    tile_count = lax.axis_size("obj")
    position_count = amplitudes.shape[0]
    width = amplitudes.shape[1]
    capacity = max(2, 2 * position_count // tile_count)
    owner_ids = owners[:, 0]
    hits = (owner_ids[:, None] == jnp.arange(tile_count, dtype=jnp.int32)[None, :]).astype(
        jnp.int32
    )
    ranks = jnp.sum((jnp.cumsum(hits, axis=0) - 1) * hits, axis=1)
    destination = owner_ids * capacity + ranks
    buffer_rows = tile_count * capacity
    marked = jnp.concatenate([offsets, jnp.ones((position_count, 1), jnp.int32)], axis=1)
    request_send = jnp.zeros((buffer_rows, 3), jnp.int32).at[destination].set(marked)
    requests = lax.all_to_all(request_send, "obj", split_axis=0, concat_axis=0, tiled=True)
    recv_corners, recv_valid = requests[:, :2], requests[:, 2]
    windows = cut_windows(object_tiles, recv_corners, width)
    arrived = lax.all_to_all(windows, "obj", split_axis=0, concat_axis=0, tiled=True)
    gradients, probe_part = run_positions(arrived[destination], amplitudes, probe_modes, phase_map)
    grad_buffer = jnp.zeros(arrived.shape, jnp.bfloat16).at[destination].set(gradients)
    returned = lax.all_to_all(grad_buffer, "obj", split_axis=0, concat_axis=0, tiled=True)
    running = accumulate(returned, recv_corners, recv_valid, object_tiles)
    probe_obj = lax.psum(probe_part, "obj")
    joined = jnp.concatenate([running.reshape(-1), probe_obj.reshape(-1)])
    joined = lax.psum(joined, "scan")
    tile_total = joined[: running.size].reshape(running.shape)
    probe_total = joined[running.size :].reshape(probe_part.shape)
    return (tile_total, probe_total)


def solution(mesh):
    placed = (
        P(None, None, "obj", None),
        P(),
        P(),
        P(("obj", "scan"), None, None),
        P(("obj", "scan"), None),
        P(("obj", "scan"), None),
    )
    return jax.shard_map(
        on_device,
        mesh=mesh,
        in_specs=placed,
        out_specs=(P(None, None, "obj", None), P()),
        check_vma=False,
    )
```

```python
import math

import jax
import numpy as np
import jax.numpy as jnp
from jax import lax
from jax.sharding import PartitionSpec as P
from jax.experimental import pallas as pl
from jax.experimental.pallas import tpu as pltpu

highest = lax.Precision.HIGHEST


def dft_tables(length):
    counter = jnp.arange(length, dtype=jnp.int32)
    product = counter[:, None] * counter[None, :] % length
    angles = product.astype(jnp.float32) * (2.0 * math.pi / length)
    scaling = 1.0 / math.sqrt(length)
    return (jnp.cos(angles) * scaling, jnp.sin(angles) * scaling)


def right_apply(real_part, imag_part, tables, inverse):
    cosine, sines = tables
    real_cos = jnp.einsum("...ij,jk->...ik", real_part, cosine, precision=highest)
    real_sin = jnp.einsum("...ij,jk->...ik", real_part, sines, precision=highest)
    imag_cos = jnp.einsum("...ij,jk->...ik", imag_part, cosine, precision=highest)
    imag_sin = jnp.einsum("...ij,jk->...ik", imag_part, sines, precision=highest)
    if inverse:
        return (real_cos - imag_sin, imag_cos + real_sin)
    return (real_cos + imag_sin, imag_cos - real_sin)


def left_apply(real_part, imag_part, tables, inverse):
    cosine, sines = tables
    real_cos = jnp.einsum("ij,...jk->...ik", cosine, real_part, precision=highest)
    real_sin = jnp.einsum("ij,...jk->...ik", sines, real_part, precision=highest)
    imag_cos = jnp.einsum("ij,...jk->...ik", cosine, imag_part, precision=highest)
    imag_sin = jnp.einsum("ij,...jk->...ik", sines, imag_part, precision=highest)
    if inverse:
        return (real_cos - imag_sin, imag_cos + real_sin)
    return (real_cos + imag_sin, imag_cos - real_sin)


def transform(real_part, imag_part, tables, inverse):
    half_re, half_im = right_apply(real_part, imag_part, tables, inverse)
    return left_apply(half_re, half_im, tables, inverse)


def complex_mul(left_re, left_im, right_re, right_im):
    return (left_re * right_re - left_im * right_im, left_re * right_im + left_im * right_re)


def position_terms(layers, measured, weights, probe_modes, kernel, tables):
    values = layers.astype(jnp.float32)
    one_re = values[:, 0, 0][:, None]
    one_im = values[:, 0, 1][:, None]
    two_re = values[:, 1, 0][:, None]
    two_im = values[:, 1, 1][:, None]
    probe_re = probe_modes[:, 0][None]
    probe_im = probe_modes[:, 1][None]
    kern_re, kern_im = kernel
    enter_re, enter_im = complex_mul(probe_re, probe_im, one_re, one_im)
    freq_re, freq_im = transform(enter_re, enter_im, tables, False)
    freq_re, freq_im = complex_mul(freq_re, freq_im, kern_re, kern_im)
    spread_re, spread_im = transform(freq_re, freq_im, tables, True)
    leave_re, leave_im = complex_mul(spread_re, spread_im, two_re, two_im)
    far_re, far_im = transform(leave_re, leave_im, tables, False)
    intensity = jnp.sum(far_re * far_re + far_im * far_im, axis=1, keepdims=True)
    factor = 1.0 - measured[:, None] / jnp.sqrt(jnp.maximum(intensity, 1.0))
    back_re, back_im = transform(far_re * factor, far_im * factor, tables, True)
    gtwo_re, gtwo_im = complex_mul(spread_re, -spread_im, back_re, back_im)
    bspread_re, bspread_im = complex_mul(two_re, -two_im, back_re, back_im)
    freq_re, freq_im = transform(bspread_re, bspread_im, tables, False)
    freq_re, freq_im = complex_mul(freq_re, freq_im, kern_re, -kern_im)
    bone_re, bone_im = transform(freq_re, freq_im, tables, True)
    gone_re, gone_im = complex_mul(probe_re, -probe_im, bone_re, bone_im)
    gprobe_re, gprobe_im = complex_mul(one_re, -one_im, bone_re, bone_im)
    slot_weight = weights.astype(jnp.float32)
    patch_weight = slot_weight[:, None, None, None, None]
    mode_weight = slot_weight[:, None, None, None]
    grad_one = jnp.stack([jnp.sum(gone_re, axis=1), jnp.sum(gone_im, axis=1)], axis=1)
    grad_two = jnp.stack([jnp.sum(gtwo_re, axis=1), jnp.sum(gtwo_im, axis=1)], axis=1)
    patch_grad = (jnp.stack([grad_one, grad_two], axis=1) * patch_weight).astype(jnp.bfloat16)
    probe_grad = jnp.stack(
        [jnp.sum(gprobe_re * mode_weight, axis=0), jnp.sum(gprobe_im * mode_weight, axis=0)], axis=1
    )
    return (patch_grad, probe_grad)


def run_slots(windows, measured, weights, probe_modes, kernel, tables):
    slot_count = windows.shape[0]
    group_size = math.gcd(slot_count, 4)
    rounds = slot_count // group_size
    grouped = (
        windows.reshape((rounds, group_size) + windows.shape[1:]),
        measured.reshape((rounds, group_size) + measured.shape[1:]),
        weights.reshape(rounds, group_size),
    )

    def one_group(members):
        group_windows, group_measured, group_weights = members

        def active(_):
            return position_terms(
                group_windows, group_measured, group_weights, probe_modes, kernel, tables
            )

        def nothing(_):
            return (
                jnp.zeros(group_windows.shape, jnp.bfloat16),
                jnp.zeros(probe_modes.shape, jnp.float32),
            )

        return lax.cond(jnp.any(group_weights > 0), active, nothing, 0)

    gradients, probe_parts = lax.map(one_group, grouped)
    return (gradients.reshape(windows.shape), jnp.sum(probe_parts, axis=0))


def split_bf16(values):
    high = values.astype(jnp.bfloat16)
    low = (values - high.astype(jnp.float32)).astype(jnp.bfloat16)
    return high, low


def stacked_tables(width):
    counter = np.arange(width)
    angles = (counter[:, None] * counter[None, :] % width) * (2.0 * np.pi / width)
    cosine = np.cos(angles) / np.sqrt(width)
    sines = np.sin(angles) / np.sqrt(width)
    forward = np.block([[cosine, -sines], [sines, cosine]])
    inverse = np.block([[cosine, sines], [-sines, cosine]])
    both = np.stack([forward, inverse])
    high = both.astype(jnp.bfloat16)
    low = (both - high.astype(np.float64)).astype(jnp.bfloat16)
    return jnp.asarray(np.stack([high, low], axis=1))


def split_dot(left, right, left_split, right_split):
    left_high, left_low = left_split(left)
    right_high, right_low = right_split(right)
    total = jnp.dot(left_high, right_high, preferred_element_type=jnp.float32)
    total = total + jnp.dot(left_low, right_high, preferred_element_type=jnp.float32)
    return total + jnp.dot(left_high, right_low, preferred_element_type=jnp.float32)


def position_kernel(rows_ref, window_ref, measured_ref, probe_ref, phase_ref, table_ref, patch_ref, probe_out_ref):
    width = measured_ref.shape[-1]
    modes = probe_ref.shape[0]

    @pl.when(pl.program_id(0) == 0)
    def _():
        probe_out_ref[...] = jnp.zeros(probe_out_ref.shape, jnp.float32)

    def table(index):
        return lambda _: (table_ref[index, 0], table_ref[index, 1])

    def transform(reals, imags, inverse):
        right_index = 1 if inverse else 0
        joined = jnp.concatenate(
            [jnp.concatenate([real, imag], axis=1) for real, imag in zip(reals, imags)], axis=0
        )
        half = split_dot(joined, None, split_bf16, table(right_index))
        stacked = jnp.concatenate(
            [
                jnp.concatenate(
                    [half[m * width:(m + 1) * width, :width], half[m * width:(m + 1) * width, width:]],
                    axis=0,
                )
                for m in range(len(reals))
            ],
            axis=1,
        )
        full = split_dot(None, stacked, table(1 - right_index), split_bf16)
        return (
            [full[:width, m * width:(m + 1) * width] for m in range(len(reals))],
            [full[width:, m * width:(m + 1) * width] for m in range(len(reals))],
        )

    def each(function, *lists):
        results = [function(*members) for members in zip(*lists)]
        return [r[0] for r in results], [r[1] for r in results]

    one_re = window_ref[0, 0, 0].astype(jnp.float32)
    one_im = window_ref[0, 0, 1].astype(jnp.float32)
    two_re = window_ref[0, 1, 0].astype(jnp.float32)
    two_im = window_ref[0, 1, 1].astype(jnp.float32)
    kern_re = phase_ref[0]
    kern_im = phase_ref[1]
    probe_re = [probe_ref[m, 0] for m in range(modes)]
    probe_im = [probe_ref[m, 1] for m in range(modes)]

    enter = each(lambda a, b: complex_mul(a, b, one_re, one_im), probe_re, probe_im)
    freq = transform(*enter, False)
    freq = each(lambda a, b: complex_mul(a, b, kern_re, kern_im), *freq)
    spread_re, spread_im = transform(*freq, True)
    leave = each(lambda a, b: complex_mul(a, b, two_re, two_im), spread_re, spread_im)
    far_re, far_im = transform(*leave, False)
    intensity = far_re[0] * far_re[0] + far_im[0] * far_im[0]
    for m in range(1, modes):
        intensity = intensity + far_re[m] * far_re[m] + far_im[m] * far_im[m]
    factor = 1.0 - measured_ref[0] / jnp.sqrt(jnp.maximum(intensity, 1.0))
    back_re, back_im = transform([f * factor for f in far_re], [f * factor for f in far_im], True)
    gtwo = each(lambda a, b, c, d: complex_mul(a, -b, c, d), spread_re, spread_im, back_re, back_im)
    bspread = each(lambda a, b: complex_mul(two_re, -two_im, a, b), back_re, back_im)
    freq = transform(*bspread, False)
    freq = each(lambda a, b: complex_mul(a, b, kern_re, -kern_im), *freq)
    bone_re, bone_im = transform(*freq, True)
    gone = each(lambda a, b, c, d: complex_mul(a, -b, c, d), probe_re, probe_im, bone_re, bone_im)
    for m in range(modes):
        term_re, term_im = complex_mul(one_re, -one_im, bone_re[m], bone_im[m])
        probe_out_ref[m, 0] = probe_out_ref[m, 0] + term_re
        probe_out_ref[m, 1] = probe_out_ref[m, 1] + term_im
    patch_ref[0, 0, 0] = sum(gone[0][1:], gone[0][0]).astype(patch_ref.dtype)
    patch_ref[0, 0, 1] = sum(gone[1][1:], gone[1][0]).astype(patch_ref.dtype)
    patch_ref[0, 1, 0] = sum(gtwo[0][1:], gtwo[0][0]).astype(patch_ref.dtype)
    patch_ref[0, 1, 1] = sum(gtwo[1][1:], gtwo[1][0]).astype(patch_ref.dtype)


def run_positions(arrived, rows, measured, probe_modes, phase_map):
    count, width = measured.shape[0], measured.shape[-1]
    modes = probe_modes.shape[0]
    tables = stacked_tables(width)
    phases = jnp.stack([jnp.cos(phase_map), jnp.sin(phase_map)])
    flops = count * modes * 6 * 2 * 3 * 2 * width * (2 * width) * (2 * width)
    row_block = (1,) + arrived.shape[1:]
    return pl.pallas_call(
        position_kernel,
        grid_spec=pltpu.PrefetchScalarGridSpec(
            num_scalar_prefetch=1,
            grid=(count,),
            in_specs=[
                pl.BlockSpec(row_block, lambda p, rows_ref: (rows_ref[p], 0, 0, 0, 0)),
                pl.BlockSpec((1, width, width), lambda p, rows_ref: (p, 0, 0)),
                pl.BlockSpec(probe_modes.shape, lambda p, rows_ref: (0, 0, 0, 0)),
                pl.BlockSpec(phases.shape, lambda p, rows_ref: (0, 0, 0)),
                pl.BlockSpec(tables.shape, lambda p, rows_ref: (0, 0, 0, 0)),
            ],
            out_specs=[
                pl.BlockSpec(row_block, lambda p, rows_ref: (rows_ref[p], 0, 0, 0, 0)),
                pl.BlockSpec(probe_modes.shape, lambda p, rows_ref: (0, 0, 0, 0)),
            ],
        ),
        out_shape=[
            jax.ShapeDtypeStruct(arrived.shape, jnp.bfloat16),
            jax.ShapeDtypeStruct(probe_modes.shape, jnp.float32),
        ],
        compiler_params=pltpu.CompilerParams(dimension_semantics=("arbitrary",)),
        cost_estimate=pl.CostEstimate(
            flops=flops, transcendentals=count * width * width, bytes_accessed=count * 6 * width * width * 4
        ),
    )(rows, arrived, measured, probe_modes, phases, tables)


def picker(size, extent, start, along_rows):
    if along_rows:
        small = lax.broadcasted_iota(jnp.int32, (size, extent), 0)
        large = lax.broadcasted_iota(jnp.int32, (size, extent), 1)
    else:
        small = lax.broadcasted_iota(jnp.int32, (extent, size), 1)
        large = lax.broadcasted_iota(jnp.int32, (extent, size), 0)
    return (large == small + start).astype(jnp.bfloat16)


def cut_kernel(request_ref, tile_ref, out_ref):
    slices, parts, extent, _ = tile_ref.shape
    width = out_ref.shape[-1]

    def one(slot, carry):
        @pl.when(request_ref[slot, 2] > 0)
        def _():
            rows = picker(width, extent, request_ref[slot, 0], True)
            cols = picker(width, extent, request_ref[slot, 1], False)
            for s in range(slices):
                for q in range(parts):
                    band = jnp.dot(rows, tile_ref[s, q], preferred_element_type=jnp.float32)
                    window = jnp.dot(band.astype(jnp.bfloat16), cols, preferred_element_type=jnp.float32)
                    out_ref[slot, s, q] = window.astype(out_ref.dtype)
        return carry

    lax.fori_loop(0, out_ref.shape[0], one, 0)


def cut_windows(local_tiles, requests, width):
    slots = requests.shape[0]
    slices, parts, extent, _ = local_tiles.shape
    return pl.pallas_call(
        cut_kernel,
        in_specs=[
            pl.BlockSpec(memory_space=pltpu.SMEM),
            pl.BlockSpec(memory_space=pltpu.VMEM),
        ],
        out_specs=pl.BlockSpec(memory_space=pltpu.VMEM),
        out_shape=jax.ShapeDtypeStruct((slots, slices, parts, width, width), jnp.bfloat16),
        cost_estimate=pl.CostEstimate(
            flops=8 * slices * parts * 2 * width * extent * (extent + width),
            transcendentals=0,
            bytes_accessed=local_tiles.size * 2 + 8 * slices * parts * width * width * 2,
        ),
    )(requests, local_tiles)


def accumulate_kernel(request_ref, grad_ref, out_ref):
    slices, parts, extent, _ = out_ref.shape
    width = grad_ref.shape[-1]
    out_ref[...] = jnp.zeros(out_ref.shape, jnp.float32)

    def one(slot, carry):
        @pl.when(request_ref[slot, 2] > 0)
        def _():
            rows = picker(width, extent, request_ref[slot, 0], False)
            cols = picker(width, extent, request_ref[slot, 1], True)
            for s in range(slices):
                for q in range(parts):
                    band = jnp.dot(grad_ref[slot, s, q], cols, preferred_element_type=jnp.float32)
                    placed = jnp.dot(rows, band.astype(jnp.bfloat16), preferred_element_type=jnp.float32)
                    out_ref[s, q] = out_ref[s, q] + placed
        return carry

    lax.fori_loop(0, grad_ref.shape[0], one, 0)


def accumulate(gradients, requests, local_tiles):
    slices, parts, extent, _ = local_tiles.shape
    width = gradients.shape[-1]
    return pl.pallas_call(
        accumulate_kernel,
        in_specs=[
            pl.BlockSpec(memory_space=pltpu.SMEM),
            pl.BlockSpec(memory_space=pltpu.VMEM),
        ],
        out_specs=pl.BlockSpec(memory_space=pltpu.VMEM),
        out_shape=jax.ShapeDtypeStruct(local_tiles.shape, jnp.float32),
        cost_estimate=pl.CostEstimate(
            flops=8 * slices * parts * 2 * width * extent * (extent + width),
            transcendentals=0,
            bytes_accessed=gradients.size * 2 + local_tiles.size * 4,
        ),
    )(requests, gradients)


def on_device(object_tiles, probe_modes, phase_map, amplitudes, offsets, owners):
    tile_count = lax.axis_size("obj")
    position_count = amplitudes.shape[0]
    width = amplitudes.shape[1]
    capacity = max(2, 2 * position_count // tile_count)
    owner_ids = owners[:, 0]
    hits = (owner_ids[:, None] == jnp.arange(tile_count, dtype=jnp.int32)[None, :]).astype(
        jnp.int32
    )
    ranks = jnp.sum((jnp.cumsum(hits, axis=0) - 1) * hits, axis=1)
    destination = owner_ids * capacity + ranks
    buffer_rows = tile_count * capacity
    marked = jnp.concatenate([offsets, jnp.ones((position_count, 1), jnp.int32)], axis=1)
    request_send = jnp.zeros((buffer_rows, 3), jnp.int32).at[destination].set(marked)
    requests = lax.all_to_all(request_send, "obj", split_axis=0, concat_axis=0, tiled=True)
    windows = cut_windows(object_tiles, requests, width)
    arrived = lax.all_to_all(windows, "obj", split_axis=0, concat_axis=0, tiled=True)
    grad_buffer, probe_part = run_positions(arrived, destination, amplitudes, probe_modes, phase_map)
    returned = lax.all_to_all(grad_buffer, "obj", split_axis=0, concat_axis=0, tiled=True)
    running = accumulate(returned, requests, object_tiles)
    probe_obj = lax.psum(probe_part, "obj")
    joined = jnp.concatenate([running.reshape(-1), probe_obj.reshape(-1)])
    joined = lax.psum(joined, "scan")
    tile_total = joined[: running.size].reshape(running.shape)
    probe_total = joined[running.size :].reshape(probe_part.shape)
    return (tile_total, probe_total)


def solution(mesh):
    placed = (
        P(None, None, "obj", None),
        P(),
        P(),
        P(("obj", "scan"), None, None),
        P(("obj", "scan"), None),
        P(("obj", "scan"), None),
    )
    return jax.shard_map(
        on_device,
        mesh=mesh,
        in_specs=placed,
        out_specs=(P(None, None, "obj", None), P()),
        check_vma=False,
    )
```

```python
import math

import jax
import numpy as np
import jax.numpy as jnp
from jax import lax
from jax.sharding import PartitionSpec as P
from jax.experimental import pallas as pl
from jax.experimental.pallas import tpu as pltpu

highest = lax.Precision.HIGHEST


def dft_tables(length):
    counter = jnp.arange(length, dtype=jnp.int32)
    product = counter[:, None] * counter[None, :] % length
    angles = product.astype(jnp.float32) * (2.0 * math.pi / length)
    scaling = 1.0 / math.sqrt(length)
    return (jnp.cos(angles) * scaling, jnp.sin(angles) * scaling)


def right_apply(real_part, imag_part, tables, inverse):
    cosine, sines = tables
    real_cos = jnp.einsum("...ij,jk->...ik", real_part, cosine, precision=highest)
    real_sin = jnp.einsum("...ij,jk->...ik", real_part, sines, precision=highest)
    imag_cos = jnp.einsum("...ij,jk->...ik", imag_part, cosine, precision=highest)
    imag_sin = jnp.einsum("...ij,jk->...ik", imag_part, sines, precision=highest)
    if inverse:
        return (real_cos - imag_sin, imag_cos + real_sin)
    return (real_cos + imag_sin, imag_cos - real_sin)


def left_apply(real_part, imag_part, tables, inverse):
    cosine, sines = tables
    real_cos = jnp.einsum("ij,...jk->...ik", cosine, real_part, precision=highest)
    real_sin = jnp.einsum("ij,...jk->...ik", sines, real_part, precision=highest)
    imag_cos = jnp.einsum("ij,...jk->...ik", cosine, imag_part, precision=highest)
    imag_sin = jnp.einsum("ij,...jk->...ik", sines, imag_part, precision=highest)
    if inverse:
        return (real_cos - imag_sin, imag_cos + real_sin)
    return (real_cos + imag_sin, imag_cos - real_sin)


def transform(real_part, imag_part, tables, inverse):
    half_re, half_im = right_apply(real_part, imag_part, tables, inverse)
    return left_apply(half_re, half_im, tables, inverse)


def complex_mul(left_re, left_im, right_re, right_im):
    return (left_re * right_re - left_im * right_im, left_re * right_im + left_im * right_re)


def position_terms(layers, measured, weights, probe_modes, kernel, tables):
    values = layers.astype(jnp.float32)
    one_re = values[:, 0, 0][:, None]
    one_im = values[:, 0, 1][:, None]
    two_re = values[:, 1, 0][:, None]
    two_im = values[:, 1, 1][:, None]
    probe_re = probe_modes[:, 0][None]
    probe_im = probe_modes[:, 1][None]
    kern_re, kern_im = kernel
    enter_re, enter_im = complex_mul(probe_re, probe_im, one_re, one_im)
    freq_re, freq_im = transform(enter_re, enter_im, tables, False)
    freq_re, freq_im = complex_mul(freq_re, freq_im, kern_re, kern_im)
    spread_re, spread_im = transform(freq_re, freq_im, tables, True)
    leave_re, leave_im = complex_mul(spread_re, spread_im, two_re, two_im)
    far_re, far_im = transform(leave_re, leave_im, tables, False)
    intensity = jnp.sum(far_re * far_re + far_im * far_im, axis=1, keepdims=True)
    factor = 1.0 - measured[:, None] / jnp.sqrt(jnp.maximum(intensity, 1.0))
    back_re, back_im = transform(far_re * factor, far_im * factor, tables, True)
    gtwo_re, gtwo_im = complex_mul(spread_re, -spread_im, back_re, back_im)
    bspread_re, bspread_im = complex_mul(two_re, -two_im, back_re, back_im)
    freq_re, freq_im = transform(bspread_re, bspread_im, tables, False)
    freq_re, freq_im = complex_mul(freq_re, freq_im, kern_re, -kern_im)
    bone_re, bone_im = transform(freq_re, freq_im, tables, True)
    gone_re, gone_im = complex_mul(probe_re, -probe_im, bone_re, bone_im)
    gprobe_re, gprobe_im = complex_mul(one_re, -one_im, bone_re, bone_im)
    slot_weight = weights.astype(jnp.float32)
    patch_weight = slot_weight[:, None, None, None, None]
    mode_weight = slot_weight[:, None, None, None]
    grad_one = jnp.stack([jnp.sum(gone_re, axis=1), jnp.sum(gone_im, axis=1)], axis=1)
    grad_two = jnp.stack([jnp.sum(gtwo_re, axis=1), jnp.sum(gtwo_im, axis=1)], axis=1)
    patch_grad = (jnp.stack([grad_one, grad_two], axis=1) * patch_weight).astype(jnp.bfloat16)
    probe_grad = jnp.stack(
        [jnp.sum(gprobe_re * mode_weight, axis=0), jnp.sum(gprobe_im * mode_weight, axis=0)], axis=1
    )
    return (patch_grad, probe_grad)


def run_slots(windows, measured, weights, probe_modes, kernel, tables):
    slot_count = windows.shape[0]
    group_size = math.gcd(slot_count, 4)
    rounds = slot_count // group_size
    grouped = (
        windows.reshape((rounds, group_size) + windows.shape[1:]),
        measured.reshape((rounds, group_size) + measured.shape[1:]),
        weights.reshape(rounds, group_size),
    )

    def one_group(members):
        group_windows, group_measured, group_weights = members

        def active(_):
            return position_terms(
                group_windows, group_measured, group_weights, probe_modes, kernel, tables
            )

        def nothing(_):
            return (
                jnp.zeros(group_windows.shape, jnp.bfloat16),
                jnp.zeros(probe_modes.shape, jnp.float32),
            )

        return lax.cond(jnp.any(group_weights > 0), active, nothing, 0)

    gradients, probe_parts = lax.map(one_group, grouped)
    return (gradients.reshape(windows.shape), jnp.sum(probe_parts, axis=0))


def split_bf16(values):
    high = values.astype(jnp.bfloat16)
    low = (values - high.astype(jnp.float32)).astype(jnp.bfloat16)
    return high, low


def stacked_tables(width):
    counter = np.arange(width)
    angles = (counter[:, None] * counter[None, :] % width) * (2.0 * np.pi / width)
    cosine = np.cos(angles) / np.sqrt(width)
    sines = np.sin(angles) / np.sqrt(width)
    forward = np.block([[cosine, -sines], [sines, cosine]])
    inverse = np.block([[cosine, sines], [-sines, cosine]])
    both = np.stack([forward, inverse])
    high = both.astype(jnp.bfloat16)
    low = (both - high.astype(np.float64)).astype(jnp.bfloat16)
    return jnp.asarray(np.stack([high, low], axis=1))


def split_dot(left, right, left_split, right_split):
    left_high, left_low = left_split(left)
    right_high, right_low = right_split(right)
    total = jnp.dot(left_high, right_high, preferred_element_type=jnp.float32)
    total = total + jnp.dot(left_low, right_high, preferred_element_type=jnp.float32)
    return total + jnp.dot(left_high, right_low, preferred_element_type=jnp.float32)


def position_kernel(rows_ref, window_ref, measured_ref, probe_ref, phase_ref, table_ref, patch_ref, probe_out_ref):
    width = measured_ref.shape[-1]
    modes = probe_ref.shape[0]

    @pl.when(pl.program_id(0) == 0)
    def _():
        probe_out_ref[...] = jnp.zeros(probe_out_ref.shape, jnp.float32)

    def table(index):
        return lambda _: (table_ref[index, 0], table_ref[index, 1])

    def transform(reals, imags, inverse):
        right_index = 1 if inverse else 0
        joined = jnp.concatenate(
            [jnp.concatenate([real, imag], axis=1) for real, imag in zip(reals, imags)], axis=0
        )
        half = split_dot(joined, None, split_bf16, table(right_index))
        stacked = jnp.concatenate(
            [
                jnp.concatenate(
                    [half[m * width:(m + 1) * width, :width], half[m * width:(m + 1) * width, width:]],
                    axis=0,
                )
                for m in range(len(reals))
            ],
            axis=1,
        )
        full = split_dot(None, stacked, table(1 - right_index), split_bf16)
        return (
            [full[:width, m * width:(m + 1) * width] for m in range(len(reals))],
            [full[width:, m * width:(m + 1) * width] for m in range(len(reals))],
        )

    def each(function, *lists):
        results = [function(*members) for members in zip(*lists)]
        return [r[0] for r in results], [r[1] for r in results]

    one_re = window_ref[0, 0, 0].astype(jnp.float32)
    one_im = window_ref[0, 0, 1].astype(jnp.float32)
    two_re = window_ref[0, 1, 0].astype(jnp.float32)
    two_im = window_ref[0, 1, 1].astype(jnp.float32)
    kern_re = phase_ref[0]
    kern_im = phase_ref[1]
    probe_re = [probe_ref[m, 0] for m in range(modes)]
    probe_im = [probe_ref[m, 1] for m in range(modes)]

    enter = each(lambda a, b: complex_mul(a, b, one_re, one_im), probe_re, probe_im)
    freq = transform(*enter, False)
    freq = each(lambda a, b: complex_mul(a, b, kern_re, kern_im), *freq)
    spread_re, spread_im = transform(*freq, True)
    leave = each(lambda a, b: complex_mul(a, b, two_re, two_im), spread_re, spread_im)
    far_re, far_im = transform(*leave, False)
    intensity = far_re[0] * far_re[0] + far_im[0] * far_im[0]
    for m in range(1, modes):
        intensity = intensity + far_re[m] * far_re[m] + far_im[m] * far_im[m]
    factor = 1.0 - measured_ref[0] / jnp.sqrt(jnp.maximum(intensity, 1.0))
    back_re, back_im = transform([f * factor for f in far_re], [f * factor for f in far_im], True)
    gtwo = each(lambda a, b, c, d: complex_mul(a, -b, c, d), spread_re, spread_im, back_re, back_im)
    bspread = each(lambda a, b: complex_mul(two_re, -two_im, a, b), back_re, back_im)
    freq = transform(*bspread, False)
    freq = each(lambda a, b: complex_mul(a, b, kern_re, -kern_im), *freq)
    bone_re, bone_im = transform(*freq, True)
    gone = each(lambda a, b, c, d: complex_mul(a, -b, c, d), probe_re, probe_im, bone_re, bone_im)
    for m in range(modes):
        term_re, term_im = complex_mul(one_re, -one_im, bone_re[m], bone_im[m])
        probe_out_ref[m, 0] = probe_out_ref[m, 0] + term_re
        probe_out_ref[m, 1] = probe_out_ref[m, 1] + term_im
    patch_ref[0, 0, 0] = sum(gone[0][1:], gone[0][0]).astype(patch_ref.dtype)
    patch_ref[0, 0, 1] = sum(gone[1][1:], gone[1][0]).astype(patch_ref.dtype)
    patch_ref[0, 1, 0] = sum(gtwo[0][1:], gtwo[0][0]).astype(patch_ref.dtype)
    patch_ref[0, 1, 1] = sum(gtwo[1][1:], gtwo[1][0]).astype(patch_ref.dtype)


def run_positions(arrived, rows, measured, probe_modes, phase_map):
    count, width = measured.shape[0], measured.shape[-1]
    modes = probe_modes.shape[0]
    tables = stacked_tables(width)
    phases = jnp.stack([jnp.cos(phase_map), jnp.sin(phase_map)])
    flops = count * modes * 6 * 2 * 3 * 2 * width * (2 * width) * (2 * width)
    row_block = (1,) + arrived.shape[1:]
    return pl.pallas_call(
        position_kernel,
        grid_spec=pltpu.PrefetchScalarGridSpec(
            num_scalar_prefetch=1,
            grid=(count,),
            in_specs=[
                pl.BlockSpec(row_block, lambda p, rows_ref: (rows_ref[p], 0, 0, 0, 0)),
                pl.BlockSpec((1, width, width), lambda p, rows_ref: (p, 0, 0)),
                pl.BlockSpec(probe_modes.shape, lambda p, rows_ref: (0, 0, 0, 0)),
                pl.BlockSpec(phases.shape, lambda p, rows_ref: (0, 0, 0)),
                pl.BlockSpec(tables.shape, lambda p, rows_ref: (0, 0, 0, 0)),
            ],
            out_specs=[
                pl.BlockSpec(row_block, lambda p, rows_ref: (rows_ref[p], 0, 0, 0, 0)),
                pl.BlockSpec(probe_modes.shape, lambda p, rows_ref: (0, 0, 0, 0)),
            ],
        ),
        out_shape=[
            jax.ShapeDtypeStruct(arrived.shape, jnp.bfloat16),
            jax.ShapeDtypeStruct(probe_modes.shape, jnp.float32),
        ],
        compiler_params=pltpu.CompilerParams(dimension_semantics=("arbitrary",)),
        cost_estimate=pl.CostEstimate(
            flops=flops, transcendentals=count * width * width, bytes_accessed=count * 6 * width * width * 4
        ),
    )(rows, arrived, measured, probe_modes, phases, tables)


def picker(size, extent, start, along_rows):
    if along_rows:
        small = lax.broadcasted_iota(jnp.int32, (size, extent), 0)
        large = lax.broadcasted_iota(jnp.int32, (size, extent), 1)
    else:
        small = lax.broadcasted_iota(jnp.int32, (extent, size), 1)
        large = lax.broadcasted_iota(jnp.int32, (extent, size), 0)
    return (large == small + start).astype(jnp.bfloat16)


def selectors(corners, width, extent):
    position = jnp.arange(width, dtype=jnp.int32)
    cells = jnp.arange(extent, dtype=jnp.int32)
    rows = cells[None, None, :] == corners[:, 0, None, None] + position[None, :, None]
    cols = cells[None, None, :] == corners[:, 1, None, None] + position[None, :, None]
    return rows.astype(jnp.bfloat16), cols.astype(jnp.bfloat16)


def cut_windows(local_tiles, corners, width):
    extent = local_tiles.shape[-1]
    rows, cols = selectors(corners, width, extent)
    picked_rows = jnp.einsum(
        "iar,skrc->iskac", rows, local_tiles, preferred_element_type=jnp.float32
    ).astype(jnp.bfloat16)
    return jnp.einsum(
        "iskac,ibc->iskab", picked_rows, cols, preferred_element_type=jnp.float32
    ).astype(jnp.bfloat16)


def accumulate_kernel(request_ref, grad_ref, out_ref):
    slices, parts, extent, _ = out_ref.shape
    width = grad_ref.shape[-1]
    out_ref[...] = jnp.zeros(out_ref.shape, jnp.float32)

    def one(slot, carry):
        @pl.when(request_ref[slot, 2] > 0)
        def _():
            rows = picker(width, extent, request_ref[slot, 0], False)
            cols = picker(width, extent, request_ref[slot, 1], True)
            for s in range(slices):
                for q in range(parts):
                    band = jnp.dot(grad_ref[slot, s, q], cols, preferred_element_type=jnp.float32)
                    placed = jnp.dot(rows, band.astype(jnp.bfloat16), preferred_element_type=jnp.float32)
                    out_ref[s, q] = out_ref[s, q] + placed
        return carry

    lax.fori_loop(0, grad_ref.shape[0], one, 0)


def accumulate(gradients, requests, local_tiles):
    slices, parts, extent, _ = local_tiles.shape
    width = gradients.shape[-1]
    return pl.pallas_call(
        accumulate_kernel,
        in_specs=[
            pl.BlockSpec(memory_space=pltpu.SMEM),
            pl.BlockSpec(memory_space=pltpu.VMEM),
        ],
        out_specs=pl.BlockSpec(memory_space=pltpu.VMEM),
        out_shape=jax.ShapeDtypeStruct(local_tiles.shape, jnp.float32),
        cost_estimate=pl.CostEstimate(
            flops=8 * slices * parts * 2 * width * extent * (extent + width),
            transcendentals=0,
            bytes_accessed=gradients.size * 2 + local_tiles.size * 4,
        ),
    )(requests, gradients)


def on_device(object_tiles, probe_modes, phase_map, amplitudes, offsets, owners):
    tile_count = lax.axis_size("obj")
    position_count = amplitudes.shape[0]
    width = amplitudes.shape[1]
    capacity = max(2, 2 * position_count // tile_count)
    owner_ids = owners[:, 0]
    hits = (owner_ids[:, None] == jnp.arange(tile_count, dtype=jnp.int32)[None, :]).astype(
        jnp.int32
    )
    ranks = jnp.sum((jnp.cumsum(hits, axis=0) - 1) * hits, axis=1)
    destination = owner_ids * capacity + ranks
    buffer_rows = tile_count * capacity
    marked = jnp.concatenate([offsets, jnp.ones((position_count, 1), jnp.int32)], axis=1)
    request_send = jnp.zeros((buffer_rows, 3), jnp.int32).at[destination].set(marked)
    requests = lax.all_to_all(request_send, "obj", split_axis=0, concat_axis=0, tiled=True)
    windows = cut_windows(object_tiles, requests[:, :2], width)
    arrived = lax.all_to_all(windows, "obj", split_axis=0, concat_axis=0, tiled=True)
    grad_buffer, probe_part = run_positions(arrived, destination, amplitudes, probe_modes, phase_map)
    returned = lax.all_to_all(grad_buffer, "obj", split_axis=0, concat_axis=0, tiled=True)
    running = accumulate(returned, requests, object_tiles)
    probe_chunks = probe_part.reshape(tile_count, -1)
    probe_piece = jnp.sum(
        lax.all_to_all(probe_chunks, "obj", split_axis=0, concat_axis=0, tiled=True), axis=0
    )
    joined = jnp.concatenate([running.reshape(-1), probe_piece])
    joined = lax.psum(joined, "scan")
    tile_total = joined[: running.size].reshape(running.shape)
    piece_total = jnp.broadcast_to(joined[running.size :][None], probe_chunks.shape)
    probe_total = lax.all_to_all(piece_total, "obj", split_axis=0, concat_axis=0, tiled=True)
    probe_total = probe_total.reshape(probe_part.shape)
    return (tile_total, probe_total)


def solution(mesh):
    placed = (
        P(None, None, "obj", None),
        P(),
        P(),
        P(("obj", "scan"), None, None),
        P(("obj", "scan"), None),
        P(("obj", "scan"), None),
    )
    return jax.shard_map(
        on_device,
        mesh=mesh,
        in_specs=placed,
        out_specs=(P(None, None, "obj", None), P()),
        check_vma=False,
    )
```

```python
import math

import jax
import numpy as np
import jax.numpy as jnp
from jax import lax
from jax.sharding import PartitionSpec as P
from jax.experimental import pallas as pl
from jax.experimental.pallas import tpu as pltpu

highest = lax.Precision.HIGHEST


def dft_tables(length):
    counter = jnp.arange(length, dtype=jnp.int32)
    product = counter[:, None] * counter[None, :] % length
    angles = product.astype(jnp.float32) * (2.0 * math.pi / length)
    scaling = 1.0 / math.sqrt(length)
    return (jnp.cos(angles) * scaling, jnp.sin(angles) * scaling)


def right_apply(real_part, imag_part, tables, inverse):
    cosine, sines = tables
    real_cos = jnp.einsum("...ij,jk->...ik", real_part, cosine, precision=highest)
    real_sin = jnp.einsum("...ij,jk->...ik", real_part, sines, precision=highest)
    imag_cos = jnp.einsum("...ij,jk->...ik", imag_part, cosine, precision=highest)
    imag_sin = jnp.einsum("...ij,jk->...ik", imag_part, sines, precision=highest)
    if inverse:
        return (real_cos - imag_sin, imag_cos + real_sin)
    return (real_cos + imag_sin, imag_cos - real_sin)


def left_apply(real_part, imag_part, tables, inverse):
    cosine, sines = tables
    real_cos = jnp.einsum("ij,...jk->...ik", cosine, real_part, precision=highest)
    real_sin = jnp.einsum("ij,...jk->...ik", sines, real_part, precision=highest)
    imag_cos = jnp.einsum("ij,...jk->...ik", cosine, imag_part, precision=highest)
    imag_sin = jnp.einsum("ij,...jk->...ik", sines, imag_part, precision=highest)
    if inverse:
        return (real_cos - imag_sin, imag_cos + real_sin)
    return (real_cos + imag_sin, imag_cos - real_sin)


def transform(real_part, imag_part, tables, inverse):
    half_re, half_im = right_apply(real_part, imag_part, tables, inverse)
    return left_apply(half_re, half_im, tables, inverse)


def complex_mul(left_re, left_im, right_re, right_im):
    return (left_re * right_re - left_im * right_im, left_re * right_im + left_im * right_re)


def position_terms(layers, measured, weights, probe_modes, kernel, tables):
    values = layers.astype(jnp.float32)
    one_re = values[:, 0, 0][:, None]
    one_im = values[:, 0, 1][:, None]
    two_re = values[:, 1, 0][:, None]
    two_im = values[:, 1, 1][:, None]
    probe_re = probe_modes[:, 0][None]
    probe_im = probe_modes[:, 1][None]
    kern_re, kern_im = kernel
    enter_re, enter_im = complex_mul(probe_re, probe_im, one_re, one_im)
    freq_re, freq_im = transform(enter_re, enter_im, tables, False)
    freq_re, freq_im = complex_mul(freq_re, freq_im, kern_re, kern_im)
    spread_re, spread_im = transform(freq_re, freq_im, tables, True)
    leave_re, leave_im = complex_mul(spread_re, spread_im, two_re, two_im)
    far_re, far_im = transform(leave_re, leave_im, tables, False)
    intensity = jnp.sum(far_re * far_re + far_im * far_im, axis=1, keepdims=True)
    factor = 1.0 - measured[:, None] / jnp.sqrt(jnp.maximum(intensity, 1.0))
    back_re, back_im = transform(far_re * factor, far_im * factor, tables, True)
    gtwo_re, gtwo_im = complex_mul(spread_re, -spread_im, back_re, back_im)
    bspread_re, bspread_im = complex_mul(two_re, -two_im, back_re, back_im)
    freq_re, freq_im = transform(bspread_re, bspread_im, tables, False)
    freq_re, freq_im = complex_mul(freq_re, freq_im, kern_re, -kern_im)
    bone_re, bone_im = transform(freq_re, freq_im, tables, True)
    gone_re, gone_im = complex_mul(probe_re, -probe_im, bone_re, bone_im)
    gprobe_re, gprobe_im = complex_mul(one_re, -one_im, bone_re, bone_im)
    slot_weight = weights.astype(jnp.float32)
    patch_weight = slot_weight[:, None, None, None, None]
    mode_weight = slot_weight[:, None, None, None]
    grad_one = jnp.stack([jnp.sum(gone_re, axis=1), jnp.sum(gone_im, axis=1)], axis=1)
    grad_two = jnp.stack([jnp.sum(gtwo_re, axis=1), jnp.sum(gtwo_im, axis=1)], axis=1)
    patch_grad = (jnp.stack([grad_one, grad_two], axis=1) * patch_weight).astype(jnp.bfloat16)
    probe_grad = jnp.stack(
        [jnp.sum(gprobe_re * mode_weight, axis=0), jnp.sum(gprobe_im * mode_weight, axis=0)], axis=1
    )
    return (patch_grad, probe_grad)


def run_slots(windows, measured, weights, probe_modes, kernel, tables):
    slot_count = windows.shape[0]
    group_size = math.gcd(slot_count, 4)
    rounds = slot_count // group_size
    grouped = (
        windows.reshape((rounds, group_size) + windows.shape[1:]),
        measured.reshape((rounds, group_size) + measured.shape[1:]),
        weights.reshape(rounds, group_size),
    )

    def one_group(members):
        group_windows, group_measured, group_weights = members

        def active(_):
            return position_terms(
                group_windows, group_measured, group_weights, probe_modes, kernel, tables
            )

        def nothing(_):
            return (
                jnp.zeros(group_windows.shape, jnp.bfloat16),
                jnp.zeros(probe_modes.shape, jnp.float32),
            )

        return lax.cond(jnp.any(group_weights > 0), active, nothing, 0)

    gradients, probe_parts = lax.map(one_group, grouped)
    return (gradients.reshape(windows.shape), jnp.sum(probe_parts, axis=0))


def split_bf16(values):
    high = values.astype(jnp.bfloat16)
    low = (values - high.astype(jnp.float32)).astype(jnp.bfloat16)
    return high, low


def stacked_tables(width):
    counter = np.arange(width)
    angles = (counter[:, None] * counter[None, :] % width) * (2.0 * np.pi / width)
    cosine = np.cos(angles) / np.sqrt(width)
    sines = np.sin(angles) / np.sqrt(width)
    forward = np.block([[cosine, -sines], [sines, cosine]])
    inverse = np.block([[cosine, sines], [-sines, cosine]])
    both = np.stack([forward, inverse])
    high = both.astype(jnp.bfloat16)
    low = (both - high.astype(np.float64)).astype(jnp.bfloat16)
    return jnp.asarray(np.stack([high, low], axis=1))


def split_dot(left, right, left_split, right_split):
    left_high, left_low = left_split(left)
    right_high, right_low = right_split(right)
    total = jnp.dot(left_high, right_high, preferred_element_type=jnp.float32)
    total = total + jnp.dot(left_low, right_high, preferred_element_type=jnp.float32)
    return total + jnp.dot(left_high, right_low, preferred_element_type=jnp.float32)


def position_kernel(rows_ref, window_ref, measured_ref, probe_ref, phase_ref, table_ref, patch_ref, probe_out_ref):
    width = measured_ref.shape[-1]
    modes = probe_ref.shape[0]

    @pl.when(pl.program_id(0) == 0)
    def _():
        probe_out_ref[...] = jnp.zeros(probe_out_ref.shape, jnp.float32)

    def table(index):
        return lambda _: (table_ref[index, 0], table_ref[index, 1])

    def transform(reals, imags, inverse):
        right_index = 1 if inverse else 0
        joined = jnp.concatenate(
            [jnp.concatenate([real, imag], axis=1) for real, imag in zip(reals, imags)], axis=0
        )
        half = split_dot(joined, None, split_bf16, table(right_index))
        stacked = jnp.concatenate(
            [
                jnp.concatenate(
                    [half[m * width:(m + 1) * width, :width], half[m * width:(m + 1) * width, width:]],
                    axis=0,
                )
                for m in range(len(reals))
            ],
            axis=1,
        )
        full = split_dot(None, stacked, table(1 - right_index), split_bf16)
        return (
            [full[:width, m * width:(m + 1) * width] for m in range(len(reals))],
            [full[width:, m * width:(m + 1) * width] for m in range(len(reals))],
        )

    def each(function, *lists):
        results = [function(*members) for members in zip(*lists)]
        return [r[0] for r in results], [r[1] for r in results]

    one_re = window_ref[0, 0, 0].astype(jnp.float32)
    one_im = window_ref[0, 0, 1].astype(jnp.float32)
    two_re = window_ref[0, 1, 0].astype(jnp.float32)
    two_im = window_ref[0, 1, 1].astype(jnp.float32)
    kern_re = phase_ref[0]
    kern_im = phase_ref[1]
    probe_re = [probe_ref[m, 0] for m in range(modes)]
    probe_im = [probe_ref[m, 1] for m in range(modes)]

    enter = each(lambda a, b: complex_mul(a, b, one_re, one_im), probe_re, probe_im)
    freq = transform(*enter, False)
    freq = each(lambda a, b: complex_mul(a, b, kern_re, kern_im), *freq)
    spread_re, spread_im = transform(*freq, True)
    leave = each(lambda a, b: complex_mul(a, b, two_re, two_im), spread_re, spread_im)
    far_re, far_im = transform(*leave, False)
    intensity = far_re[0] * far_re[0] + far_im[0] * far_im[0]
    for m in range(1, modes):
        intensity = intensity + far_re[m] * far_re[m] + far_im[m] * far_im[m]
    factor = 1.0 - measured_ref[0] / jnp.sqrt(jnp.maximum(intensity, 1.0))
    back_re, back_im = transform([f * factor for f in far_re], [f * factor for f in far_im], True)
    gtwo = each(lambda a, b, c, d: complex_mul(a, -b, c, d), spread_re, spread_im, back_re, back_im)
    bspread = each(lambda a, b: complex_mul(two_re, -two_im, a, b), back_re, back_im)
    freq = transform(*bspread, False)
    freq = each(lambda a, b: complex_mul(a, b, kern_re, -kern_im), *freq)
    bone_re, bone_im = transform(*freq, True)
    gone = each(lambda a, b, c, d: complex_mul(a, -b, c, d), probe_re, probe_im, bone_re, bone_im)
    for m in range(modes):
        term_re, term_im = complex_mul(one_re, -one_im, bone_re[m], bone_im[m])
        probe_out_ref[m, 0] = probe_out_ref[m, 0] + term_re
        probe_out_ref[m, 1] = probe_out_ref[m, 1] + term_im
    patch_ref[0, 0, 0] = sum(gone[0][1:], gone[0][0]).astype(patch_ref.dtype)
    patch_ref[0, 0, 1] = sum(gone[1][1:], gone[1][0]).astype(patch_ref.dtype)
    patch_ref[0, 1, 0] = sum(gtwo[0][1:], gtwo[0][0]).astype(patch_ref.dtype)
    patch_ref[0, 1, 1] = sum(gtwo[1][1:], gtwo[1][0]).astype(patch_ref.dtype)


def run_positions(arrived, rows, measured, probe_modes, phase_map):
    count, width = measured.shape[0], measured.shape[-1]
    modes = probe_modes.shape[0]
    tables = stacked_tables(width)
    phases = jnp.stack([jnp.cos(phase_map), jnp.sin(phase_map)])
    flops = count * modes * 6 * 2 * 3 * 2 * width * (2 * width) * (2 * width)
    row_block = (1,) + arrived.shape[1:]
    return pl.pallas_call(
        position_kernel,
        grid_spec=pltpu.PrefetchScalarGridSpec(
            num_scalar_prefetch=1,
            grid=(count,),
            in_specs=[
                pl.BlockSpec(row_block, lambda p, rows_ref: (rows_ref[p], 0, 0, 0, 0)),
                pl.BlockSpec((1, width, width), lambda p, rows_ref: (p, 0, 0)),
                pl.BlockSpec(probe_modes.shape, lambda p, rows_ref: (0, 0, 0, 0)),
                pl.BlockSpec(phases.shape, lambda p, rows_ref: (0, 0, 0)),
                pl.BlockSpec(tables.shape, lambda p, rows_ref: (0, 0, 0, 0)),
            ],
            out_specs=[
                pl.BlockSpec(row_block, lambda p, rows_ref: (rows_ref[p], 0, 0, 0, 0)),
                pl.BlockSpec(probe_modes.shape, lambda p, rows_ref: (0, 0, 0, 0)),
            ],
        ),
        out_shape=[
            jax.ShapeDtypeStruct(arrived.shape, jnp.bfloat16),
            jax.ShapeDtypeStruct(probe_modes.shape, jnp.float32),
        ],
        compiler_params=pltpu.CompilerParams(dimension_semantics=("arbitrary",)),
        cost_estimate=pl.CostEstimate(
            flops=flops, transcendentals=count * width * width, bytes_accessed=count * 6 * width * width * 4
        ),
    )(rows, arrived, measured, probe_modes, phases, tables)


def picker(size, extent, start, along_rows):
    if along_rows:
        small = lax.broadcasted_iota(jnp.int32, (size, extent), 0)
        large = lax.broadcasted_iota(jnp.int32, (size, extent), 1)
    else:
        small = lax.broadcasted_iota(jnp.int32, (extent, size), 1)
        large = lax.broadcasted_iota(jnp.int32, (extent, size), 0)
    return (large == small + start).astype(jnp.bfloat16)


def cut_kernel(request_ref, tile_ref, out_ref, stage_ref, copy_sem):
    slices, parts, extent, _ = tile_ref.shape
    width = out_ref.shape[-1]

    def one(slot, carry):
        @pl.when(request_ref[slot, 2] > 0)
        def _():
            rows = picker(width, extent, request_ref[slot, 0], True)
            cols = picker(width, extent, request_ref[slot, 1], False)
            for s in range(slices):
                for q in range(parts):
                    band = jnp.dot(rows, tile_ref[s, q], preferred_element_type=jnp.float32)
                    window = jnp.dot(band.astype(jnp.bfloat16), cols, preferred_element_type=jnp.float32)
                    stage_ref[s, q] = window.astype(stage_ref.dtype)
            copy = pltpu.make_async_copy(stage_ref, out_ref.at[slot], copy_sem)
            copy.start()
            copy.wait()
        return carry

    lax.fori_loop(0, out_ref.shape[0], one, 0)


def cut_windows(local_tiles, requests, width):
    slots = requests.shape[0]
    slices, parts, extent, _ = local_tiles.shape
    return pl.pallas_call(
        cut_kernel,
        in_specs=[
            pl.BlockSpec(memory_space=pltpu.SMEM),
            pl.BlockSpec(memory_space=pltpu.VMEM),
        ],
        out_specs=pl.BlockSpec(memory_space=pl.ANY),
        out_shape=jax.ShapeDtypeStruct((slots, slices, parts, width, width), jnp.bfloat16),
        scratch_shapes=[
            pltpu.VMEM((slices, parts, width, width), jnp.bfloat16),
            pltpu.SemaphoreType.DMA,
        ],
        cost_estimate=pl.CostEstimate(
            flops=8 * slices * parts * 2 * width * extent * (extent + width),
            transcendentals=0,
            bytes_accessed=local_tiles.size * 2 + 8 * slices * parts * width * width * 2,
        ),
    )(requests, local_tiles)


def accumulate_kernel(request_ref, grad_ref, out_ref):
    slices, parts, extent, _ = out_ref.shape
    width = grad_ref.shape[-1]
    out_ref[...] = jnp.zeros(out_ref.shape, jnp.float32)

    def one(slot, carry):
        @pl.when(request_ref[slot, 2] > 0)
        def _():
            rows = picker(width, extent, request_ref[slot, 0], False)
            cols = picker(width, extent, request_ref[slot, 1], True)
            for s in range(slices):
                for q in range(parts):
                    band = jnp.dot(grad_ref[slot, s, q], cols, preferred_element_type=jnp.float32)
                    placed = jnp.dot(rows, band.astype(jnp.bfloat16), preferred_element_type=jnp.float32)
                    out_ref[s, q] = out_ref[s, q] + placed
        return carry

    lax.fori_loop(0, grad_ref.shape[0], one, 0)


def accumulate(gradients, requests, local_tiles):
    slices, parts, extent, _ = local_tiles.shape
    width = gradients.shape[-1]
    return pl.pallas_call(
        accumulate_kernel,
        in_specs=[
            pl.BlockSpec(memory_space=pltpu.SMEM),
            pl.BlockSpec(memory_space=pltpu.VMEM),
        ],
        out_specs=pl.BlockSpec(memory_space=pltpu.VMEM),
        out_shape=jax.ShapeDtypeStruct(local_tiles.shape, jnp.float32),
        cost_estimate=pl.CostEstimate(
            flops=8 * slices * parts * 2 * width * extent * (extent + width),
            transcendentals=0,
            bytes_accessed=gradients.size * 2 + local_tiles.size * 4,
        ),
    )(requests, gradients)


def on_device(object_tiles, probe_modes, phase_map, amplitudes, offsets, owners):
    tile_count = lax.axis_size("obj")
    position_count = amplitudes.shape[0]
    width = amplitudes.shape[1]
    capacity = max(2, 2 * position_count // tile_count)
    owner_ids = owners[:, 0]
    hits = (owner_ids[:, None] == jnp.arange(tile_count, dtype=jnp.int32)[None, :]).astype(
        jnp.int32
    )
    ranks = jnp.sum((jnp.cumsum(hits, axis=0) - 1) * hits, axis=1)
    destination = owner_ids * capacity + ranks
    buffer_rows = tile_count * capacity
    marked = jnp.concatenate([offsets, jnp.ones((position_count, 1), jnp.int32)], axis=1)
    request_send = jnp.zeros((buffer_rows, 3), jnp.int32).at[destination].set(marked)
    requests = lax.all_to_all(request_send, "obj", split_axis=0, concat_axis=0, tiled=True)
    windows = cut_windows(object_tiles, requests, width)
    arrived = lax.all_to_all(windows, "obj", split_axis=0, concat_axis=0, tiled=True)
    grad_buffer, probe_part = run_positions(arrived, destination, amplitudes, probe_modes, phase_map)
    returned = lax.all_to_all(grad_buffer, "obj", split_axis=0, concat_axis=0, tiled=True)
    running = accumulate(returned, requests, object_tiles)
    probe_chunks = probe_part.reshape(tile_count, -1)
    probe_piece = jnp.sum(
        lax.all_to_all(probe_chunks, "obj", split_axis=0, concat_axis=0, tiled=True), axis=0
    )
    joined = jnp.concatenate([running.reshape(-1), probe_piece])
    joined = lax.psum(joined, "scan")
    tile_total = joined[: running.size].reshape(running.shape)
    piece_total = jnp.broadcast_to(joined[running.size :][None], probe_chunks.shape)
    probe_total = lax.all_to_all(piece_total, "obj", split_axis=0, concat_axis=0, tiled=True)
    probe_total = probe_total.reshape(probe_part.shape)
    return (tile_total, probe_total)


def solution(mesh):
    placed = (
        P(None, None, "obj", None),
        P(),
        P(),
        P(("obj", "scan"), None, None),
        P(("obj", "scan"), None),
        P(("obj", "scan"), None),
    )
    return jax.shard_map(
        on_device,
        mesh=mesh,
        in_specs=placed,
        out_specs=(P(None, None, "obj", None), P()),
        check_vma=False,
    )
```

```python
import math

import jax
import numpy as np
import jax.numpy as jnp
from jax import lax
from jax.sharding import PartitionSpec as P
from jax.experimental import pallas as pl
from jax.experimental.pallas import tpu as pltpu

highest = lax.Precision.HIGHEST


def dft_tables(length):
    counter = jnp.arange(length, dtype=jnp.int32)
    product = counter[:, None] * counter[None, :] % length
    angles = product.astype(jnp.float32) * (2.0 * math.pi / length)
    scaling = 1.0 / math.sqrt(length)
    return (jnp.cos(angles) * scaling, jnp.sin(angles) * scaling)


def right_apply(real_part, imag_part, tables, inverse):
    cosine, sines = tables
    real_cos = jnp.einsum("...ij,jk->...ik", real_part, cosine, precision=highest)
    real_sin = jnp.einsum("...ij,jk->...ik", real_part, sines, precision=highest)
    imag_cos = jnp.einsum("...ij,jk->...ik", imag_part, cosine, precision=highest)
    imag_sin = jnp.einsum("...ij,jk->...ik", imag_part, sines, precision=highest)
    if inverse:
        return (real_cos - imag_sin, imag_cos + real_sin)
    return (real_cos + imag_sin, imag_cos - real_sin)


def left_apply(real_part, imag_part, tables, inverse):
    cosine, sines = tables
    real_cos = jnp.einsum("ij,...jk->...ik", cosine, real_part, precision=highest)
    real_sin = jnp.einsum("ij,...jk->...ik", sines, real_part, precision=highest)
    imag_cos = jnp.einsum("ij,...jk->...ik", cosine, imag_part, precision=highest)
    imag_sin = jnp.einsum("ij,...jk->...ik", sines, imag_part, precision=highest)
    if inverse:
        return (real_cos - imag_sin, imag_cos + real_sin)
    return (real_cos + imag_sin, imag_cos - real_sin)


def transform(real_part, imag_part, tables, inverse):
    half_re, half_im = right_apply(real_part, imag_part, tables, inverse)
    return left_apply(half_re, half_im, tables, inverse)


def complex_mul(left_re, left_im, right_re, right_im):
    return (left_re * right_re - left_im * right_im, left_re * right_im + left_im * right_re)


def position_terms(layers, measured, weights, probe_modes, kernel, tables):
    values = layers.astype(jnp.float32)
    one_re = values[:, 0, 0][:, None]
    one_im = values[:, 0, 1][:, None]
    two_re = values[:, 1, 0][:, None]
    two_im = values[:, 1, 1][:, None]
    probe_re = probe_modes[:, 0][None]
    probe_im = probe_modes[:, 1][None]
    kern_re, kern_im = kernel
    enter_re, enter_im = complex_mul(probe_re, probe_im, one_re, one_im)
    freq_re, freq_im = transform(enter_re, enter_im, tables, False)
    freq_re, freq_im = complex_mul(freq_re, freq_im, kern_re, kern_im)
    spread_re, spread_im = transform(freq_re, freq_im, tables, True)
    leave_re, leave_im = complex_mul(spread_re, spread_im, two_re, two_im)
    far_re, far_im = transform(leave_re, leave_im, tables, False)
    intensity = jnp.sum(far_re * far_re + far_im * far_im, axis=1, keepdims=True)
    factor = 1.0 - measured[:, None] / jnp.sqrt(jnp.maximum(intensity, 1.0))
    back_re, back_im = transform(far_re * factor, far_im * factor, tables, True)
    gtwo_re, gtwo_im = complex_mul(spread_re, -spread_im, back_re, back_im)
    bspread_re, bspread_im = complex_mul(two_re, -two_im, back_re, back_im)
    freq_re, freq_im = transform(bspread_re, bspread_im, tables, False)
    freq_re, freq_im = complex_mul(freq_re, freq_im, kern_re, -kern_im)
    bone_re, bone_im = transform(freq_re, freq_im, tables, True)
    gone_re, gone_im = complex_mul(probe_re, -probe_im, bone_re, bone_im)
    gprobe_re, gprobe_im = complex_mul(one_re, -one_im, bone_re, bone_im)
    slot_weight = weights.astype(jnp.float32)
    patch_weight = slot_weight[:, None, None, None, None]
    mode_weight = slot_weight[:, None, None, None]
    grad_one = jnp.stack([jnp.sum(gone_re, axis=1), jnp.sum(gone_im, axis=1)], axis=1)
    grad_two = jnp.stack([jnp.sum(gtwo_re, axis=1), jnp.sum(gtwo_im, axis=1)], axis=1)
    patch_grad = (jnp.stack([grad_one, grad_two], axis=1) * patch_weight).astype(jnp.bfloat16)
    probe_grad = jnp.stack(
        [jnp.sum(gprobe_re * mode_weight, axis=0), jnp.sum(gprobe_im * mode_weight, axis=0)], axis=1
    )
    return (patch_grad, probe_grad)


def run_slots(windows, measured, weights, probe_modes, kernel, tables):
    slot_count = windows.shape[0]
    group_size = math.gcd(slot_count, 4)
    rounds = slot_count // group_size
    grouped = (
        windows.reshape((rounds, group_size) + windows.shape[1:]),
        measured.reshape((rounds, group_size) + measured.shape[1:]),
        weights.reshape(rounds, group_size),
    )

    def one_group(members):
        group_windows, group_measured, group_weights = members

        def active(_):
            return position_terms(
                group_windows, group_measured, group_weights, probe_modes, kernel, tables
            )

        def nothing(_):
            return (
                jnp.zeros(group_windows.shape, jnp.bfloat16),
                jnp.zeros(probe_modes.shape, jnp.float32),
            )

        return lax.cond(jnp.any(group_weights > 0), active, nothing, 0)

    gradients, probe_parts = lax.map(one_group, grouped)
    return (gradients.reshape(windows.shape), jnp.sum(probe_parts, axis=0))


def split_bf16(values):
    high = values.astype(jnp.bfloat16)
    low = (values - high.astype(jnp.float32)).astype(jnp.bfloat16)
    return high, low


def stacked_tables(width):
    counter = np.arange(width)
    angles = (counter[:, None] * counter[None, :] % width) * (2.0 * np.pi / width)
    cosine = np.cos(angles) / np.sqrt(width)
    sines = np.sin(angles) / np.sqrt(width)
    forward = np.block([[cosine, -sines], [sines, cosine]])
    inverse = np.block([[cosine, sines], [-sines, cosine]])
    both = np.stack([forward, inverse])
    high = both.astype(jnp.bfloat16)
    low = (both - high.astype(np.float64)).astype(jnp.bfloat16)
    return jnp.asarray(np.stack([high, low], axis=1))


def split_dot(left, right, left_split, right_split):
    left_high, left_low = left_split(left)
    right_high, right_low = right_split(right)
    total = jnp.dot(left_high, right_high, preferred_element_type=jnp.float32)
    total = total + jnp.dot(left_low, right_high, preferred_element_type=jnp.float32)
    return total + jnp.dot(left_high, right_low, preferred_element_type=jnp.float32)


def position_kernel(rows_ref, window_ref, measured_ref, probe_ref, phase_ref, table_ref, patch_ref, probe_out_ref):
    width = measured_ref.shape[-1]
    modes = probe_ref.shape[0]

    @pl.when(pl.program_id(0) == 0)
    def _():
        probe_out_ref[...] = jnp.zeros(probe_out_ref.shape, jnp.float32)

    def table(index):
        return lambda _: (table_ref[index, 0], table_ref[index, 1])

    def transform(reals, imags, inverse):
        right_index = 1 if inverse else 0
        joined = jnp.concatenate(
            [jnp.concatenate([real, imag], axis=1) for real, imag in zip(reals, imags)], axis=0
        )
        half = split_dot(joined, None, split_bf16, table(right_index))
        stacked = jnp.concatenate(
            [
                jnp.concatenate(
                    [half[m * width:(m + 1) * width, :width], half[m * width:(m + 1) * width, width:]],
                    axis=0,
                )
                for m in range(len(reals))
            ],
            axis=1,
        )
        full = split_dot(None, stacked, table(1 - right_index), split_bf16)
        return (
            [full[:width, m * width:(m + 1) * width] for m in range(len(reals))],
            [full[width:, m * width:(m + 1) * width] for m in range(len(reals))],
        )

    def each(function, *lists):
        results = [function(*members) for members in zip(*lists)]
        return [r[0] for r in results], [r[1] for r in results]

    one_re = window_ref[0, 0, 0].astype(jnp.float32)
    one_im = window_ref[0, 0, 1].astype(jnp.float32)
    two_re = window_ref[0, 1, 0].astype(jnp.float32)
    two_im = window_ref[0, 1, 1].astype(jnp.float32)
    kern_re = phase_ref[0]
    kern_im = phase_ref[1]
    probe_re = [probe_ref[m, 0] for m in range(modes)]
    probe_im = [probe_ref[m, 1] for m in range(modes)]

    enter = each(lambda a, b: complex_mul(a, b, one_re, one_im), probe_re, probe_im)
    freq = transform(*enter, False)
    freq = each(lambda a, b: complex_mul(a, b, kern_re, kern_im), *freq)
    spread_re, spread_im = transform(*freq, True)
    leave = each(lambda a, b: complex_mul(a, b, two_re, two_im), spread_re, spread_im)
    far_re, far_im = transform(*leave, False)
    intensity = far_re[0] * far_re[0] + far_im[0] * far_im[0]
    for m in range(1, modes):
        intensity = intensity + far_re[m] * far_re[m] + far_im[m] * far_im[m]
    factor = 1.0 - measured_ref[0] / jnp.sqrt(jnp.maximum(intensity, 1.0))
    back_re, back_im = transform([f * factor for f in far_re], [f * factor for f in far_im], True)
    gtwo = each(lambda a, b, c, d: complex_mul(a, -b, c, d), spread_re, spread_im, back_re, back_im)
    bspread = each(lambda a, b: complex_mul(two_re, -two_im, a, b), back_re, back_im)
    freq = transform(*bspread, False)
    freq = each(lambda a, b: complex_mul(a, b, kern_re, -kern_im), *freq)
    bone_re, bone_im = transform(*freq, True)
    gone = each(lambda a, b, c, d: complex_mul(a, -b, c, d), probe_re, probe_im, bone_re, bone_im)
    for m in range(modes):
        term_re, term_im = complex_mul(one_re, -one_im, bone_re[m], bone_im[m])
        probe_out_ref[m, 0] = probe_out_ref[m, 0] + term_re
        probe_out_ref[m, 1] = probe_out_ref[m, 1] + term_im
    patch_ref[0, 0, 0] = sum(gone[0][1:], gone[0][0]).astype(patch_ref.dtype)
    patch_ref[0, 0, 1] = sum(gone[1][1:], gone[1][0]).astype(patch_ref.dtype)
    patch_ref[0, 1, 0] = sum(gtwo[0][1:], gtwo[0][0]).astype(patch_ref.dtype)
    patch_ref[0, 1, 1] = sum(gtwo[1][1:], gtwo[1][0]).astype(patch_ref.dtype)


def run_positions(arrived, rows, measured, probe_modes, phase_map):
    count, width = measured.shape[0], measured.shape[-1]
    modes = probe_modes.shape[0]
    tables = stacked_tables(width)
    phases = jnp.stack([jnp.cos(phase_map), jnp.sin(phase_map)])
    flops = count * modes * 6 * 2 * 3 * 2 * width * (2 * width) * (2 * width)
    row_block = (1,) + arrived.shape[1:]
    return pl.pallas_call(
        position_kernel,
        grid_spec=pltpu.PrefetchScalarGridSpec(
            num_scalar_prefetch=1,
            grid=(count,),
            in_specs=[
                pl.BlockSpec(row_block, lambda p, rows_ref: (rows_ref[p], 0, 0, 0, 0)),
                pl.BlockSpec((1, width, width), lambda p, rows_ref: (p, 0, 0)),
                pl.BlockSpec(probe_modes.shape, lambda p, rows_ref: (0, 0, 0, 0)),
                pl.BlockSpec(phases.shape, lambda p, rows_ref: (0, 0, 0)),
                pl.BlockSpec(tables.shape, lambda p, rows_ref: (0, 0, 0, 0)),
            ],
            out_specs=[
                pl.BlockSpec(row_block, lambda p, rows_ref: (rows_ref[p], 0, 0, 0, 0)),
                pl.BlockSpec(probe_modes.shape, lambda p, rows_ref: (0, 0, 0, 0)),
            ],
        ),
        out_shape=[
            jax.ShapeDtypeStruct(arrived.shape, jnp.bfloat16),
            jax.ShapeDtypeStruct(probe_modes.shape, jnp.float32),
        ],
        compiler_params=pltpu.CompilerParams(dimension_semantics=("arbitrary",)),
        cost_estimate=pl.CostEstimate(
            flops=flops, transcendentals=count * width * width, bytes_accessed=count * 6 * width * width * 4
        ),
    )(rows, arrived, measured, probe_modes, phases, tables)


def picker(size, extent, start, along_rows):
    if along_rows:
        small = lax.broadcasted_iota(jnp.int32, (size, extent), 0)
        large = lax.broadcasted_iota(jnp.int32, (size, extent), 1)
    else:
        small = lax.broadcasted_iota(jnp.int32, (extent, size), 1)
        large = lax.broadcasted_iota(jnp.int32, (extent, size), 0)
    return (large == small + start).astype(jnp.bfloat16)


def selectors(corners, width, extent):
    position = jnp.arange(width, dtype=jnp.int32)
    cells = jnp.arange(extent, dtype=jnp.int32)
    rows = cells[None, None, :] == corners[:, 0, None, None] + position[None, :, None]
    cols = cells[None, None, :] == corners[:, 1, None, None] + position[None, :, None]
    return rows.astype(jnp.bfloat16), cols.astype(jnp.bfloat16)


def cut_windows(local_tiles, corners, width):
    extent = local_tiles.shape[-1]
    rows, cols = selectors(corners, width, extent)
    picked_rows = jnp.einsum(
        "iar,skrc->iskac", rows, local_tiles, preferred_element_type=jnp.float32
    ).astype(jnp.bfloat16)
    return jnp.einsum(
        "iskac,ibc->iskab", picked_rows, cols, preferred_element_type=jnp.float32
    ).astype(jnp.bfloat16)


def accumulate_kernel(request_ref, grad_ref, out_ref):
    slices, parts, extent, _ = out_ref.shape
    width = grad_ref.shape[-1]
    out_ref[...] = jnp.zeros(out_ref.shape, jnp.float32)

    def one(slot, carry):
        @pl.when(request_ref[slot, 2] > 0)
        def _():
            top = request_ref[slot, 0]
            reach = width + 8
            start = pl.multiple_of(jnp.minimum(top // 8 * 8, extent - reach), 8)
            shift = picker(width, reach, top - start, False)
            cols = picker(width, extent, request_ref[slot, 1], True)
            for s in range(slices):
                for q in range(parts):
                    band = jnp.dot(grad_ref[slot, s, q], cols, preferred_element_type=jnp.float32)
                    placed = jnp.dot(shift, band.astype(jnp.bfloat16), preferred_element_type=jnp.float32)
                    out_ref[s, q, pl.ds(start, reach), :] = out_ref[s, q, pl.ds(start, reach), :] + placed
        return carry

    lax.fori_loop(0, grad_ref.shape[0], one, 0)


def accumulate(gradients, requests, local_tiles):
    slices, parts, extent, _ = local_tiles.shape
    width = gradients.shape[-1]
    return pl.pallas_call(
        accumulate_kernel,
        in_specs=[
            pl.BlockSpec(memory_space=pltpu.SMEM),
            pl.BlockSpec(memory_space=pltpu.VMEM),
        ],
        out_specs=pl.BlockSpec(memory_space=pltpu.VMEM),
        out_shape=jax.ShapeDtypeStruct(local_tiles.shape, jnp.float32),
        cost_estimate=pl.CostEstimate(
            flops=8 * slices * parts * 2 * width * extent * (extent + width),
            transcendentals=0,
            bytes_accessed=gradients.size * 2 + local_tiles.size * 4,
        ),
    )(requests, gradients)


def on_device(object_tiles, probe_modes, phase_map, amplitudes, offsets, owners):
    tile_count = lax.axis_size("obj")
    position_count = amplitudes.shape[0]
    width = amplitudes.shape[1]
    capacity = max(2, 2 * position_count // tile_count)
    owner_ids = owners[:, 0]
    hits = (owner_ids[:, None] == jnp.arange(tile_count, dtype=jnp.int32)[None, :]).astype(
        jnp.int32
    )
    ranks = jnp.sum((jnp.cumsum(hits, axis=0) - 1) * hits, axis=1)
    destination = owner_ids * capacity + ranks
    buffer_rows = tile_count * capacity
    marked = jnp.concatenate([offsets, jnp.ones((position_count, 1), jnp.int32)], axis=1)
    request_send = jnp.zeros((buffer_rows, 3), jnp.int32).at[destination].set(marked)
    requests = lax.all_to_all(request_send, "obj", split_axis=0, concat_axis=0, tiled=True)
    windows = cut_windows(object_tiles, requests[:, :2], width)
    arrived = lax.all_to_all(windows, "obj", split_axis=0, concat_axis=0, tiled=True)
    grad_buffer, probe_part = run_positions(arrived, destination, amplitudes, probe_modes, phase_map)
    returned = lax.all_to_all(grad_buffer, "obj", split_axis=0, concat_axis=0, tiled=True)
    running = accumulate(returned, requests, object_tiles)
    probe_scan = lax.psum(probe_part, "scan")
    running, probe_scan = lax.optimization_barrier((running, probe_scan))
    tile_total = lax.psum(running, "scan")
    probe_chunks = probe_scan.reshape(tile_count, -1)
    probe_piece = jnp.sum(
        lax.all_to_all(probe_chunks, "obj", split_axis=0, concat_axis=0, tiled=True), axis=0
    )
    piece_total = jnp.broadcast_to(probe_piece[None], probe_chunks.shape)
    probe_total = lax.all_to_all(piece_total, "obj", split_axis=0, concat_axis=0, tiled=True)
    probe_total = probe_total.reshape(probe_part.shape)
    return (tile_total, probe_total)


def solution(mesh):
    placed = (
        P(None, None, "obj", None),
        P(),
        P(),
        P(("obj", "scan"), None, None),
        P(("obj", "scan"), None),
        P(("obj", "scan"), None),
    )
    return jax.shard_map(
        on_device,
        mesh=mesh,
        in_specs=placed,
        out_specs=(P(None, None, "obj", None), P()),
        check_vma=False,
    )
```

```python
import math

import jax
import numpy as np
import jax.numpy as jnp
from jax import lax
from jax.sharding import PartitionSpec as P
from jax.experimental import pallas as pl
from jax.experimental.pallas import tpu as pltpu

highest = lax.Precision.HIGHEST


def dft_tables(length):
    counter = jnp.arange(length, dtype=jnp.int32)
    product = counter[:, None] * counter[None, :] % length
    angles = product.astype(jnp.float32) * (2.0 * math.pi / length)
    scaling = 1.0 / math.sqrt(length)
    return (jnp.cos(angles) * scaling, jnp.sin(angles) * scaling)


def right_apply(real_part, imag_part, tables, inverse):
    cosine, sines = tables
    real_cos = jnp.einsum("...ij,jk->...ik", real_part, cosine, precision=highest)
    real_sin = jnp.einsum("...ij,jk->...ik", real_part, sines, precision=highest)
    imag_cos = jnp.einsum("...ij,jk->...ik", imag_part, cosine, precision=highest)
    imag_sin = jnp.einsum("...ij,jk->...ik", imag_part, sines, precision=highest)
    if inverse:
        return (real_cos - imag_sin, imag_cos + real_sin)
    return (real_cos + imag_sin, imag_cos - real_sin)


def left_apply(real_part, imag_part, tables, inverse):
    cosine, sines = tables
    real_cos = jnp.einsum("ij,...jk->...ik", cosine, real_part, precision=highest)
    real_sin = jnp.einsum("ij,...jk->...ik", sines, real_part, precision=highest)
    imag_cos = jnp.einsum("ij,...jk->...ik", cosine, imag_part, precision=highest)
    imag_sin = jnp.einsum("ij,...jk->...ik", sines, imag_part, precision=highest)
    if inverse:
        return (real_cos - imag_sin, imag_cos + real_sin)
    return (real_cos + imag_sin, imag_cos - real_sin)


def transform(real_part, imag_part, tables, inverse):
    half_re, half_im = right_apply(real_part, imag_part, tables, inverse)
    return left_apply(half_re, half_im, tables, inverse)


def complex_mul(left_re, left_im, right_re, right_im):
    return (left_re * right_re - left_im * right_im, left_re * right_im + left_im * right_re)


def position_terms(layers, measured, weights, probe_modes, kernel, tables):
    values = layers.astype(jnp.float32)
    one_re = values[:, 0, 0][:, None]
    one_im = values[:, 0, 1][:, None]
    two_re = values[:, 1, 0][:, None]
    two_im = values[:, 1, 1][:, None]
    probe_re = probe_modes[:, 0][None]
    probe_im = probe_modes[:, 1][None]
    kern_re, kern_im = kernel
    enter_re, enter_im = complex_mul(probe_re, probe_im, one_re, one_im)
    freq_re, freq_im = transform(enter_re, enter_im, tables, False)
    freq_re, freq_im = complex_mul(freq_re, freq_im, kern_re, kern_im)
    spread_re, spread_im = transform(freq_re, freq_im, tables, True)
    leave_re, leave_im = complex_mul(spread_re, spread_im, two_re, two_im)
    far_re, far_im = transform(leave_re, leave_im, tables, False)
    intensity = jnp.sum(far_re * far_re + far_im * far_im, axis=1, keepdims=True)
    factor = 1.0 - measured[:, None] / jnp.sqrt(jnp.maximum(intensity, 1.0))
    back_re, back_im = transform(far_re * factor, far_im * factor, tables, True)
    gtwo_re, gtwo_im = complex_mul(spread_re, -spread_im, back_re, back_im)
    bspread_re, bspread_im = complex_mul(two_re, -two_im, back_re, back_im)
    freq_re, freq_im = transform(bspread_re, bspread_im, tables, False)
    freq_re, freq_im = complex_mul(freq_re, freq_im, kern_re, -kern_im)
    bone_re, bone_im = transform(freq_re, freq_im, tables, True)
    gone_re, gone_im = complex_mul(probe_re, -probe_im, bone_re, bone_im)
    gprobe_re, gprobe_im = complex_mul(one_re, -one_im, bone_re, bone_im)
    slot_weight = weights.astype(jnp.float32)
    patch_weight = slot_weight[:, None, None, None, None]
    mode_weight = slot_weight[:, None, None, None]
    grad_one = jnp.stack([jnp.sum(gone_re, axis=1), jnp.sum(gone_im, axis=1)], axis=1)
    grad_two = jnp.stack([jnp.sum(gtwo_re, axis=1), jnp.sum(gtwo_im, axis=1)], axis=1)
    patch_grad = (jnp.stack([grad_one, grad_two], axis=1) * patch_weight).astype(jnp.bfloat16)
    probe_grad = jnp.stack(
        [jnp.sum(gprobe_re * mode_weight, axis=0), jnp.sum(gprobe_im * mode_weight, axis=0)], axis=1
    )
    return (patch_grad, probe_grad)


def run_slots(windows, measured, weights, probe_modes, kernel, tables):
    slot_count = windows.shape[0]
    group_size = math.gcd(slot_count, 4)
    rounds = slot_count // group_size
    grouped = (
        windows.reshape((rounds, group_size) + windows.shape[1:]),
        measured.reshape((rounds, group_size) + measured.shape[1:]),
        weights.reshape(rounds, group_size),
    )

    def one_group(members):
        group_windows, group_measured, group_weights = members

        def active(_):
            return position_terms(
                group_windows, group_measured, group_weights, probe_modes, kernel, tables
            )

        def nothing(_):
            return (
                jnp.zeros(group_windows.shape, jnp.bfloat16),
                jnp.zeros(probe_modes.shape, jnp.float32),
            )

        return lax.cond(jnp.any(group_weights > 0), active, nothing, 0)

    gradients, probe_parts = lax.map(one_group, grouped)
    return (gradients.reshape(windows.shape), jnp.sum(probe_parts, axis=0))


def split_bf16(values):
    high = values.astype(jnp.bfloat16)
    low = (values - high.astype(jnp.float32)).astype(jnp.bfloat16)
    return high, low


def stacked_tables(width):
    counter = np.arange(width)
    angles = (counter[:, None] * counter[None, :] % width) * (2.0 * np.pi / width)
    cosine = np.cos(angles) / np.sqrt(width)
    sines = np.sin(angles) / np.sqrt(width)
    forward = np.block([[cosine, -sines], [sines, cosine]])
    inverse = np.block([[cosine, sines], [-sines, cosine]])
    both = np.stack([forward, inverse])
    high = both.astype(jnp.bfloat16)
    low = (both - high.astype(np.float64)).astype(jnp.bfloat16)
    return jnp.asarray(np.stack([high, low], axis=1))


def split_dot(left, right, left_split, right_split):
    left_high, left_low = left_split(left)
    right_high, right_low = right_split(right)
    total = jnp.dot(left_high, right_high, preferred_element_type=jnp.float32)
    total = total + jnp.dot(left_low, right_high, preferred_element_type=jnp.float32)
    return total + jnp.dot(left_high, right_low, preferred_element_type=jnp.float32)


def position_kernel(rows_ref, window_ref, measured_ref, probe_ref, phase_ref, table_ref, patch_ref, probe_out_ref):
    width = measured_ref.shape[-1]
    modes = probe_ref.shape[0]

    @pl.when(pl.program_id(0) == 0)
    def _():
        probe_out_ref[...] = jnp.zeros(probe_out_ref.shape, jnp.float32)

    def table(index):
        return lambda _: (table_ref[index, 0], table_ref[index, 1])

    def transform(reals, imags, inverse):
        right_index = 1 if inverse else 0
        joined = jnp.concatenate(
            [jnp.concatenate([real, imag], axis=1) for real, imag in zip(reals, imags)], axis=0
        )
        half = split_dot(joined, None, split_bf16, table(right_index))
        stacked = jnp.concatenate(
            [
                jnp.concatenate(
                    [half[m * width:(m + 1) * width, :width], half[m * width:(m + 1) * width, width:]],
                    axis=0,
                )
                for m in range(len(reals))
            ],
            axis=1,
        )
        full = split_dot(None, stacked, table(1 - right_index), split_bf16)
        return (
            [full[:width, m * width:(m + 1) * width] for m in range(len(reals))],
            [full[width:, m * width:(m + 1) * width] for m in range(len(reals))],
        )

    def each(function, *lists):
        results = [function(*members) for members in zip(*lists)]
        return [r[0] for r in results], [r[1] for r in results]

    one_re = window_ref[0, 0, 0].astype(jnp.float32)
    one_im = window_ref[0, 0, 1].astype(jnp.float32)
    two_re = window_ref[0, 1, 0].astype(jnp.float32)
    two_im = window_ref[0, 1, 1].astype(jnp.float32)
    kern_re = phase_ref[0]
    kern_im = phase_ref[1]
    probe_re = [probe_ref[m, 0] for m in range(modes)]
    probe_im = [probe_ref[m, 1] for m in range(modes)]

    enter = each(lambda a, b: complex_mul(a, b, one_re, one_im), probe_re, probe_im)
    freq = transform(*enter, False)
    freq = each(lambda a, b: complex_mul(a, b, kern_re, kern_im), *freq)
    spread_re, spread_im = transform(*freq, True)
    leave = each(lambda a, b: complex_mul(a, b, two_re, two_im), spread_re, spread_im)
    far_re, far_im = transform(*leave, False)
    intensity = far_re[0] * far_re[0] + far_im[0] * far_im[0]
    for m in range(1, modes):
        intensity = intensity + far_re[m] * far_re[m] + far_im[m] * far_im[m]
    factor = 1.0 - measured_ref[0] / jnp.sqrt(jnp.maximum(intensity, 1.0))
    back_re, back_im = transform([f * factor for f in far_re], [f * factor for f in far_im], True)
    gtwo = each(lambda a, b, c, d: complex_mul(a, -b, c, d), spread_re, spread_im, back_re, back_im)
    bspread = each(lambda a, b: complex_mul(two_re, -two_im, a, b), back_re, back_im)
    freq = transform(*bspread, False)
    freq = each(lambda a, b: complex_mul(a, b, kern_re, -kern_im), *freq)
    bone_re, bone_im = transform(*freq, True)
    gone = each(lambda a, b, c, d: complex_mul(a, -b, c, d), probe_re, probe_im, bone_re, bone_im)
    for m in range(modes):
        term_re, term_im = complex_mul(one_re, -one_im, bone_re[m], bone_im[m])
        probe_out_ref[m, 0] = probe_out_ref[m, 0] + term_re
        probe_out_ref[m, 1] = probe_out_ref[m, 1] + term_im
    patch_ref[0, 0, 0] = sum(gone[0][1:], gone[0][0]).astype(patch_ref.dtype)
    patch_ref[0, 0, 1] = sum(gone[1][1:], gone[1][0]).astype(patch_ref.dtype)
    patch_ref[0, 1, 0] = sum(gtwo[0][1:], gtwo[0][0]).astype(patch_ref.dtype)
    patch_ref[0, 1, 1] = sum(gtwo[1][1:], gtwo[1][0]).astype(patch_ref.dtype)


def run_positions(arrived, rows, measured, probe_modes, phase_map):
    count, width = measured.shape[0], measured.shape[-1]
    modes = probe_modes.shape[0]
    tables = stacked_tables(width)
    phases = jnp.stack([jnp.cos(phase_map), jnp.sin(phase_map)])
    flops = count * modes * 6 * 2 * 3 * 2 * width * (2 * width) * (2 * width)
    row_block = (1,) + arrived.shape[1:]
    return pl.pallas_call(
        position_kernel,
        grid_spec=pltpu.PrefetchScalarGridSpec(
            num_scalar_prefetch=1,
            grid=(count,),
            in_specs=[
                pl.BlockSpec(row_block, lambda p, rows_ref: (rows_ref[p], 0, 0, 0, 0)),
                pl.BlockSpec((1, width, width), lambda p, rows_ref: (p, 0, 0)),
                pl.BlockSpec(probe_modes.shape, lambda p, rows_ref: (0, 0, 0, 0)),
                pl.BlockSpec(phases.shape, lambda p, rows_ref: (0, 0, 0)),
                pl.BlockSpec(tables.shape, lambda p, rows_ref: (0, 0, 0, 0)),
            ],
            out_specs=[
                pl.BlockSpec(row_block, lambda p, rows_ref: (rows_ref[p], 0, 0, 0, 0)),
                pl.BlockSpec(probe_modes.shape, lambda p, rows_ref: (0, 0, 0, 0)),
            ],
        ),
        out_shape=[
            jax.ShapeDtypeStruct(arrived.shape, jnp.bfloat16),
            jax.ShapeDtypeStruct(probe_modes.shape, jnp.float32),
        ],
        compiler_params=pltpu.CompilerParams(dimension_semantics=("arbitrary",)),
        cost_estimate=pl.CostEstimate(
            flops=flops, transcendentals=count * width * width, bytes_accessed=count * 6 * width * width * 4
        ),
    )(rows, arrived, measured, probe_modes, phases, tables)


def picker(size, extent, start, along_rows):
    if along_rows:
        small = lax.broadcasted_iota(jnp.int32, (size, extent), 0)
        large = lax.broadcasted_iota(jnp.int32, (size, extent), 1)
    else:
        small = lax.broadcasted_iota(jnp.int32, (extent, size), 1)
        large = lax.broadcasted_iota(jnp.int32, (extent, size), 0)
    return (large == small + start).astype(jnp.bfloat16)


def selectors(corners, width, extent):
    position = jnp.arange(width, dtype=jnp.int32)
    cells = jnp.arange(extent, dtype=jnp.int32)
    rows = cells[None, None, :] == corners[:, 0, None, None] + position[None, :, None]
    cols = cells[None, None, :] == corners[:, 1, None, None] + position[None, :, None]
    return rows.astype(jnp.bfloat16), cols.astype(jnp.bfloat16)


def cut_windows(local_tiles, corners, width):
    extent = local_tiles.shape[-1]
    rows, cols = selectors(corners, width, extent)
    picked_rows = jnp.einsum(
        "iar,skrc->iskac", rows, local_tiles, preferred_element_type=jnp.float32
    ).astype(jnp.bfloat16)
    return jnp.einsum(
        "iskac,ibc->iskab", picked_rows, cols, preferred_element_type=jnp.float32
    ).astype(jnp.bfloat16)


def accumulate_kernel(request_ref, grad_ref, out_ref):
    slices, parts, extent, _ = out_ref.shape
    width = grad_ref.shape[-1]
    out_ref[...] = jnp.zeros(out_ref.shape, jnp.float32)

    def one(slot, carry):
        @pl.when(request_ref[slot, 2] > 0)
        def _():
            top = request_ref[slot, 0]
            reach = width + 8
            start = pl.multiple_of(jnp.minimum(top // 8 * 8, extent - reach), 8)
            shift = picker(width, reach, top - start, False)
            cols = picker(width, extent, request_ref[slot, 1], True)
            planes = [(s, q) for s in range(slices) for q in range(parts)]
            stacked = jnp.concatenate([grad_ref[slot, s, q] for s, q in planes], axis=0)
            band = jnp.dot(stacked, cols, preferred_element_type=jnp.float32).astype(jnp.bfloat16)
            wide = jnp.concatenate(
                [band[k * width:(k + 1) * width] for k in range(len(planes))], axis=1
            )
            placed = jnp.dot(shift, wide, preferred_element_type=jnp.float32)
            for k, (s, q) in enumerate(planes):
                out_ref[s, q, pl.ds(start, reach), :] = (
                    out_ref[s, q, pl.ds(start, reach), :] + placed[:, k * extent:(k + 1) * extent]
                )
        return carry

    lax.fori_loop(0, grad_ref.shape[0], one, 0)


def accumulate(gradients, requests, local_tiles):
    slices, parts, extent, _ = local_tiles.shape
    width = gradients.shape[-1]
    return pl.pallas_call(
        accumulate_kernel,
        in_specs=[
            pl.BlockSpec(memory_space=pltpu.SMEM),
            pl.BlockSpec(memory_space=pltpu.VMEM),
        ],
        out_specs=pl.BlockSpec(memory_space=pltpu.VMEM),
        out_shape=jax.ShapeDtypeStruct(local_tiles.shape, jnp.float32),
        cost_estimate=pl.CostEstimate(
            flops=8 * slices * parts * 2 * width * extent * (extent + width),
            transcendentals=0,
            bytes_accessed=gradients.size * 2 + local_tiles.size * 4,
        ),
    )(requests, gradients)


def on_device(object_tiles, probe_modes, phase_map, amplitudes, offsets, owners):
    tile_count = lax.axis_size("obj")
    position_count = amplitudes.shape[0]
    width = amplitudes.shape[1]
    capacity = max(2, 2 * position_count // tile_count)
    owner_ids = owners[:, 0]
    hits = (owner_ids[:, None] == jnp.arange(tile_count, dtype=jnp.int32)[None, :]).astype(
        jnp.int32
    )
    ranks = jnp.sum((jnp.cumsum(hits, axis=0) - 1) * hits, axis=1)
    destination = owner_ids * capacity + ranks
    buffer_rows = tile_count * capacity
    marked = jnp.concatenate([offsets, jnp.ones((position_count, 1), jnp.int32)], axis=1)
    request_send = jnp.zeros((buffer_rows, 3), jnp.int32).at[destination].set(marked)
    requests = lax.all_to_all(request_send, "obj", split_axis=0, concat_axis=0, tiled=True)
    windows = cut_windows(object_tiles, requests[:, :2], width)
    arrived = lax.all_to_all(windows, "obj", split_axis=0, concat_axis=0, tiled=True)
    grad_buffer, probe_part = run_positions(arrived, destination, amplitudes, probe_modes, phase_map)
    returned = lax.all_to_all(grad_buffer, "obj", split_axis=0, concat_axis=0, tiled=True)
    running = accumulate(returned, requests, object_tiles)
    probe_scan = lax.psum(probe_part, "scan")
    running, probe_scan = lax.optimization_barrier((running, probe_scan))
    tile_total = lax.psum(running, "scan")
    probe_chunks = probe_scan.reshape(tile_count, -1)
    probe_piece = jnp.sum(
        lax.all_to_all(probe_chunks, "obj", split_axis=0, concat_axis=0, tiled=True), axis=0
    )
    piece_total = jnp.broadcast_to(probe_piece[None], probe_chunks.shape)
    probe_total = lax.all_to_all(piece_total, "obj", split_axis=0, concat_axis=0, tiled=True)
    probe_total = probe_total.reshape(probe_part.shape)
    return (tile_total, probe_total)


def solution(mesh):
    placed = (
        P(None, None, "obj", None),
        P(),
        P(),
        P(("obj", "scan"), None, None),
        P(("obj", "scan"), None),
        P(("obj", "scan"), None),
    )
    return jax.shard_map(
        on_device,
        mesh=mesh,
        in_specs=placed,
        out_specs=(P(None, None, "obj", None), P()),
        check_vma=False,
    )
```

```python
import math

import jax
import numpy as np
import jax.numpy as jnp
from jax import lax
from jax.sharding import PartitionSpec as P
from jax.experimental import pallas as pl
from jax.experimental.pallas import tpu as pltpu

highest = lax.Precision.HIGHEST


def dft_tables(length):
    counter = jnp.arange(length, dtype=jnp.int32)
    product = counter[:, None] * counter[None, :] % length
    angles = product.astype(jnp.float32) * (2.0 * math.pi / length)
    scaling = 1.0 / math.sqrt(length)
    return (jnp.cos(angles) * scaling, jnp.sin(angles) * scaling)


def right_apply(real_part, imag_part, tables, inverse):
    cosine, sines = tables
    real_cos = jnp.einsum("...ij,jk->...ik", real_part, cosine, precision=highest)
    real_sin = jnp.einsum("...ij,jk->...ik", real_part, sines, precision=highest)
    imag_cos = jnp.einsum("...ij,jk->...ik", imag_part, cosine, precision=highest)
    imag_sin = jnp.einsum("...ij,jk->...ik", imag_part, sines, precision=highest)
    if inverse:
        return (real_cos - imag_sin, imag_cos + real_sin)
    return (real_cos + imag_sin, imag_cos - real_sin)


def left_apply(real_part, imag_part, tables, inverse):
    cosine, sines = tables
    real_cos = jnp.einsum("ij,...jk->...ik", cosine, real_part, precision=highest)
    real_sin = jnp.einsum("ij,...jk->...ik", sines, real_part, precision=highest)
    imag_cos = jnp.einsum("ij,...jk->...ik", cosine, imag_part, precision=highest)
    imag_sin = jnp.einsum("ij,...jk->...ik", sines, imag_part, precision=highest)
    if inverse:
        return (real_cos - imag_sin, imag_cos + real_sin)
    return (real_cos + imag_sin, imag_cos - real_sin)


def transform(real_part, imag_part, tables, inverse):
    half_re, half_im = right_apply(real_part, imag_part, tables, inverse)
    return left_apply(half_re, half_im, tables, inverse)


def complex_mul(left_re, left_im, right_re, right_im):
    return (left_re * right_re - left_im * right_im, left_re * right_im + left_im * right_re)


def position_terms(layers, measured, weights, probe_modes, kernel, tables):
    values = layers.astype(jnp.float32)
    one_re = values[:, 0, 0][:, None]
    one_im = values[:, 0, 1][:, None]
    two_re = values[:, 1, 0][:, None]
    two_im = values[:, 1, 1][:, None]
    probe_re = probe_modes[:, 0][None]
    probe_im = probe_modes[:, 1][None]
    kern_re, kern_im = kernel
    enter_re, enter_im = complex_mul(probe_re, probe_im, one_re, one_im)
    freq_re, freq_im = transform(enter_re, enter_im, tables, False)
    freq_re, freq_im = complex_mul(freq_re, freq_im, kern_re, kern_im)
    spread_re, spread_im = transform(freq_re, freq_im, tables, True)
    leave_re, leave_im = complex_mul(spread_re, spread_im, two_re, two_im)
    far_re, far_im = transform(leave_re, leave_im, tables, False)
    intensity = jnp.sum(far_re * far_re + far_im * far_im, axis=1, keepdims=True)
    factor = 1.0 - measured[:, None] / jnp.sqrt(jnp.maximum(intensity, 1.0))
    back_re, back_im = transform(far_re * factor, far_im * factor, tables, True)
    gtwo_re, gtwo_im = complex_mul(spread_re, -spread_im, back_re, back_im)
    bspread_re, bspread_im = complex_mul(two_re, -two_im, back_re, back_im)
    freq_re, freq_im = transform(bspread_re, bspread_im, tables, False)
    freq_re, freq_im = complex_mul(freq_re, freq_im, kern_re, -kern_im)
    bone_re, bone_im = transform(freq_re, freq_im, tables, True)
    gone_re, gone_im = complex_mul(probe_re, -probe_im, bone_re, bone_im)
    gprobe_re, gprobe_im = complex_mul(one_re, -one_im, bone_re, bone_im)
    slot_weight = weights.astype(jnp.float32)
    patch_weight = slot_weight[:, None, None, None, None]
    mode_weight = slot_weight[:, None, None, None]
    grad_one = jnp.stack([jnp.sum(gone_re, axis=1), jnp.sum(gone_im, axis=1)], axis=1)
    grad_two = jnp.stack([jnp.sum(gtwo_re, axis=1), jnp.sum(gtwo_im, axis=1)], axis=1)
    patch_grad = (jnp.stack([grad_one, grad_two], axis=1) * patch_weight).astype(jnp.bfloat16)
    probe_grad = jnp.stack(
        [jnp.sum(gprobe_re * mode_weight, axis=0), jnp.sum(gprobe_im * mode_weight, axis=0)], axis=1
    )
    return (patch_grad, probe_grad)


def run_slots(windows, measured, weights, probe_modes, kernel, tables):
    slot_count = windows.shape[0]
    group_size = math.gcd(slot_count, 4)
    rounds = slot_count // group_size
    grouped = (
        windows.reshape((rounds, group_size) + windows.shape[1:]),
        measured.reshape((rounds, group_size) + measured.shape[1:]),
        weights.reshape(rounds, group_size),
    )

    def one_group(members):
        group_windows, group_measured, group_weights = members

        def active(_):
            return position_terms(
                group_windows, group_measured, group_weights, probe_modes, kernel, tables
            )

        def nothing(_):
            return (
                jnp.zeros(group_windows.shape, jnp.bfloat16),
                jnp.zeros(probe_modes.shape, jnp.float32),
            )

        return lax.cond(jnp.any(group_weights > 0), active, nothing, 0)

    gradients, probe_parts = lax.map(one_group, grouped)
    return (gradients.reshape(windows.shape), jnp.sum(probe_parts, axis=0))


def split_bf16(values):
    high = values.astype(jnp.bfloat16)
    low = (values - high.astype(jnp.float32)).astype(jnp.bfloat16)
    return high, low


def stacked_tables(width):
    counter = np.arange(width)
    angles = (counter[:, None] * counter[None, :] % width) * (2.0 * np.pi / width)
    cosine = np.cos(angles) / np.sqrt(width)
    sines = np.sin(angles) / np.sqrt(width)
    forward = np.block([[cosine, -sines], [sines, cosine]])
    inverse = np.block([[cosine, sines], [-sines, cosine]])
    both = np.stack([forward, inverse])
    high = both.astype(jnp.bfloat16)
    low = (both - high.astype(np.float64)).astype(jnp.bfloat16)
    return jnp.asarray(np.stack([high, low], axis=1))


def split_dot(left, right, left_split, right_split):
    left_high, left_low = left_split(left)
    right_high, right_low = right_split(right)
    total = jnp.dot(left_high, right_high, preferred_element_type=jnp.float32)
    total = total + jnp.dot(left_low, right_high, preferred_element_type=jnp.float32)
    return total + jnp.dot(left_high, right_low, preferred_element_type=jnp.float32)


def position_kernel(rows_ref, window_ref, measured_ref, probe_ref, phase_ref, table_ref, patch_ref, probe_out_ref):
    width = measured_ref.shape[-1]
    modes = probe_ref.shape[0]

    @pl.when(pl.program_id(0) == 0)
    def _():
        probe_out_ref[...] = jnp.zeros(probe_out_ref.shape, jnp.float32)

    def table(index):
        return lambda _: (table_ref[index, 0], table_ref[index, 1])

    def transform(reals, imags, inverse):
        right_index = 1 if inverse else 0
        joined = jnp.concatenate(
            [jnp.concatenate([real, imag], axis=1) for real, imag in zip(reals, imags)], axis=0
        )
        half = split_dot(joined, None, split_bf16, table(right_index))
        stacked = jnp.concatenate(
            [
                jnp.concatenate(
                    [half[m * width:(m + 1) * width, :width], half[m * width:(m + 1) * width, width:]],
                    axis=0,
                )
                for m in range(len(reals))
            ],
            axis=1,
        )
        full = split_dot(None, stacked, table(1 - right_index), split_bf16)
        return (
            [full[:width, m * width:(m + 1) * width] for m in range(len(reals))],
            [full[width:, m * width:(m + 1) * width] for m in range(len(reals))],
        )

    def each(function, *lists):
        results = [function(*members) for members in zip(*lists)]
        return [r[0] for r in results], [r[1] for r in results]

    one_re = window_ref[0, 0, 0].astype(jnp.float32)
    one_im = window_ref[0, 0, 1].astype(jnp.float32)
    two_re = window_ref[0, 1, 0].astype(jnp.float32)
    two_im = window_ref[0, 1, 1].astype(jnp.float32)
    kern_re = phase_ref[0]
    kern_im = phase_ref[1]
    probe_re = [probe_ref[m, 0] for m in range(modes)]
    probe_im = [probe_ref[m, 1] for m in range(modes)]

    enter = each(lambda a, b: complex_mul(a, b, one_re, one_im), probe_re, probe_im)
    freq = transform(*enter, False)
    freq = each(lambda a, b: complex_mul(a, b, kern_re, kern_im), *freq)
    spread_re, spread_im = transform(*freq, True)
    leave = each(lambda a, b: complex_mul(a, b, two_re, two_im), spread_re, spread_im)
    far_re, far_im = transform(*leave, False)
    intensity = far_re[0] * far_re[0] + far_im[0] * far_im[0]
    for m in range(1, modes):
        intensity = intensity + far_re[m] * far_re[m] + far_im[m] * far_im[m]
    factor = 1.0 - measured_ref[0] / jnp.sqrt(jnp.maximum(intensity, 1.0))
    back_re, back_im = transform([f * factor for f in far_re], [f * factor for f in far_im], True)
    gtwo = each(lambda a, b, c, d: complex_mul(a, -b, c, d), spread_re, spread_im, back_re, back_im)
    bspread = each(lambda a, b: complex_mul(two_re, -two_im, a, b), back_re, back_im)
    freq = transform(*bspread, False)
    freq = each(lambda a, b: complex_mul(a, b, kern_re, -kern_im), *freq)
    bone_re, bone_im = transform(*freq, True)
    gone = each(lambda a, b, c, d: complex_mul(a, -b, c, d), probe_re, probe_im, bone_re, bone_im)
    for m in range(modes):
        term_re, term_im = complex_mul(one_re, -one_im, bone_re[m], bone_im[m])
        probe_out_ref[m, 0] = probe_out_ref[m, 0] + term_re
        probe_out_ref[m, 1] = probe_out_ref[m, 1] + term_im
    patch_ref[0, 0, 0] = sum(gone[0][1:], gone[0][0]).astype(patch_ref.dtype)
    patch_ref[0, 0, 1] = sum(gone[1][1:], gone[1][0]).astype(patch_ref.dtype)
    patch_ref[0, 1, 0] = sum(gtwo[0][1:], gtwo[0][0]).astype(patch_ref.dtype)
    patch_ref[0, 1, 1] = sum(gtwo[1][1:], gtwo[1][0]).astype(patch_ref.dtype)


def run_positions(arrived, rows, measured, probe_modes, phase_map):
    count, width = measured.shape[0], measured.shape[-1]
    modes = probe_modes.shape[0]
    tables = stacked_tables(width)
    phases = jnp.stack([jnp.cos(phase_map), jnp.sin(phase_map)])
    flops = count * modes * 6 * 2 * 3 * 2 * width * (2 * width) * (2 * width)
    row_block = (1,) + arrived.shape[1:]
    return pl.pallas_call(
        position_kernel,
        grid_spec=pltpu.PrefetchScalarGridSpec(
            num_scalar_prefetch=1,
            grid=(count,),
            in_specs=[
                pl.BlockSpec(row_block, lambda p, rows_ref: (rows_ref[p], 0, 0, 0, 0)),
                pl.BlockSpec((1, width, width), lambda p, rows_ref: (p, 0, 0)),
                pl.BlockSpec(probe_modes.shape, lambda p, rows_ref: (0, 0, 0, 0)),
                pl.BlockSpec(phases.shape, lambda p, rows_ref: (0, 0, 0)),
                pl.BlockSpec(tables.shape, lambda p, rows_ref: (0, 0, 0, 0)),
            ],
            out_specs=[
                pl.BlockSpec(row_block, lambda p, rows_ref: (rows_ref[p], 0, 0, 0, 0)),
                pl.BlockSpec(probe_modes.shape, lambda p, rows_ref: (0, 0, 0, 0)),
            ],
        ),
        out_shape=[
            jax.ShapeDtypeStruct(arrived.shape, jnp.bfloat16),
            jax.ShapeDtypeStruct(probe_modes.shape, jnp.float32),
        ],
        compiler_params=pltpu.CompilerParams(dimension_semantics=("arbitrary",)),
        cost_estimate=pl.CostEstimate(
            flops=flops, transcendentals=count * width * width, bytes_accessed=count * 6 * width * width * 4
        ),
    )(rows, arrived, measured, probe_modes, phases, tables)


def picker(size, extent, start, along_rows):
    if along_rows:
        small = lax.broadcasted_iota(jnp.int32, (size, extent), 0)
        large = lax.broadcasted_iota(jnp.int32, (size, extent), 1)
    else:
        small = lax.broadcasted_iota(jnp.int32, (extent, size), 1)
        large = lax.broadcasted_iota(jnp.int32, (extent, size), 0)
    return (large == small + start).astype(jnp.bfloat16)


def selectors(corners, width, extent):
    position = jnp.arange(width, dtype=jnp.int32)
    cells = jnp.arange(extent, dtype=jnp.int32)
    rows = cells[None, None, :] == corners[:, 0, None, None] + position[None, :, None]
    cols = cells[None, None, :] == corners[:, 1, None, None] + position[None, :, None]
    return rows.astype(jnp.bfloat16), cols.astype(jnp.bfloat16)


def cut_windows(local_tiles, corners, width):
    extent = local_tiles.shape[-1]
    rows, cols = selectors(corners, width, extent)
    picked_rows = jnp.einsum(
        "iar,skrc->iskac", rows, local_tiles, preferred_element_type=jnp.float32
    ).astype(jnp.bfloat16)
    return jnp.einsum(
        "iskac,ibc->iskab", picked_rows, cols, preferred_element_type=jnp.float32
    ).astype(jnp.bfloat16)


def accumulate_kernel(request_ref, grad_ref, out_ref):
    slices, parts, extent, _ = out_ref.shape
    width = grad_ref.shape[-1]
    out_ref[...] = jnp.zeros(out_ref.shape, jnp.float32)

    def one(slot, carry):
        @pl.when(request_ref[slot, 2] > 0)
        def _():
            top = request_ref[slot, 0]
            reach = width + 8
            start = pl.multiple_of(jnp.minimum(top // 8 * 8, extent - reach), 8)
            shift = picker(width, reach, top - start, False)
            left = request_ref[slot, 1]
            span = 2 * width
            first = pl.multiple_of(jnp.minimum(left // width * width, extent - span), width)
            cols = picker(width, span, left - first, True)
            planes = [(s, q) for s in range(slices) for q in range(parts)]
            stacked = jnp.concatenate([grad_ref[slot, s, q] for s, q in planes], axis=0)
            band = jnp.dot(stacked, cols, preferred_element_type=jnp.float32).astype(jnp.bfloat16)
            wide = jnp.concatenate(
                [band[k * width:(k + 1) * width] for k in range(len(planes))], axis=1
            )
            placed = jnp.dot(shift, wide, preferred_element_type=jnp.float32)
            for k, (s, q) in enumerate(planes):
                out_ref[s, q, pl.ds(start, reach), pl.ds(first, span)] = (
                    out_ref[s, q, pl.ds(start, reach), pl.ds(first, span)]
                    + placed[:, k * span:(k + 1) * span]
                )
        return carry

    lax.fori_loop(0, grad_ref.shape[0], one, 0)


def accumulate(gradients, requests, local_tiles):
    slices, parts, extent, _ = local_tiles.shape
    width = gradients.shape[-1]
    return pl.pallas_call(
        accumulate_kernel,
        in_specs=[
            pl.BlockSpec(memory_space=pltpu.SMEM),
            pl.BlockSpec(memory_space=pltpu.VMEM),
        ],
        out_specs=pl.BlockSpec(memory_space=pltpu.VMEM),
        out_shape=jax.ShapeDtypeStruct(local_tiles.shape, jnp.float32),
        cost_estimate=pl.CostEstimate(
            flops=8 * slices * parts * 2 * width * extent * (extent + width),
            transcendentals=0,
            bytes_accessed=gradients.size * 2 + local_tiles.size * 4,
        ),
    )(requests, gradients)


def on_device(object_tiles, probe_modes, phase_map, amplitudes, offsets, owners):
    tile_count = lax.axis_size("obj")
    position_count = amplitudes.shape[0]
    width = amplitudes.shape[1]
    capacity = max(2, 2 * position_count // tile_count)
    owner_ids = owners[:, 0]
    hits = (owner_ids[:, None] == jnp.arange(tile_count, dtype=jnp.int32)[None, :]).astype(
        jnp.int32
    )
    ranks = jnp.sum((jnp.cumsum(hits, axis=0) - 1) * hits, axis=1)
    destination = owner_ids * capacity + ranks
    buffer_rows = tile_count * capacity
    marked = jnp.concatenate([offsets, jnp.ones((position_count, 1), jnp.int32)], axis=1)
    request_send = jnp.zeros((buffer_rows, 3), jnp.int32).at[destination].set(marked)
    requests = lax.all_to_all(request_send, "obj", split_axis=0, concat_axis=0, tiled=True)
    windows = cut_windows(object_tiles, requests[:, :2], width)
    arrived = lax.all_to_all(windows, "obj", split_axis=0, concat_axis=0, tiled=True)
    grad_buffer, probe_part = run_positions(arrived, destination, amplitudes, probe_modes, phase_map)
    returned = lax.all_to_all(grad_buffer, "obj", split_axis=0, concat_axis=0, tiled=True)
    running = accumulate(returned, requests, object_tiles)
    probe_scan = lax.psum(probe_part, "scan")
    running, probe_scan = lax.optimization_barrier((running, probe_scan))
    tile_total = lax.psum(running, "scan")
    probe_chunks = probe_scan.reshape(tile_count, -1)
    probe_piece = jnp.sum(
        lax.all_to_all(probe_chunks, "obj", split_axis=0, concat_axis=0, tiled=True), axis=0
    )
    piece_total = jnp.broadcast_to(probe_piece[None], probe_chunks.shape)
    probe_total = lax.all_to_all(piece_total, "obj", split_axis=0, concat_axis=0, tiled=True)
    probe_total = probe_total.reshape(probe_part.shape)
    return (tile_total, probe_total)


def solution(mesh):
    placed = (
        P(None, None, "obj", None),
        P(),
        P(),
        P(("obj", "scan"), None, None),
        P(("obj", "scan"), None),
        P(("obj", "scan"), None),
    )
    return jax.shard_map(
        on_device,
        mesh=mesh,
        in_specs=placed,
        out_specs=(P(None, None, "obj", None), P()),
        check_vma=False,
    )
```

```python
import math

import jax
import numpy as np
import jax.numpy as jnp
from jax import lax
from jax.sharding import PartitionSpec as P
from jax.experimental import pallas as pl
from jax.experimental.pallas import tpu as pltpu

highest = lax.Precision.HIGHEST


def dft_tables(length):
    counter = jnp.arange(length, dtype=jnp.int32)
    product = counter[:, None] * counter[None, :] % length
    angles = product.astype(jnp.float32) * (2.0 * math.pi / length)
    scaling = 1.0 / math.sqrt(length)
    return (jnp.cos(angles) * scaling, jnp.sin(angles) * scaling)


def right_apply(real_part, imag_part, tables, inverse):
    cosine, sines = tables
    real_cos = jnp.einsum("...ij,jk->...ik", real_part, cosine, precision=highest)
    real_sin = jnp.einsum("...ij,jk->...ik", real_part, sines, precision=highest)
    imag_cos = jnp.einsum("...ij,jk->...ik", imag_part, cosine, precision=highest)
    imag_sin = jnp.einsum("...ij,jk->...ik", imag_part, sines, precision=highest)
    if inverse:
        return (real_cos - imag_sin, imag_cos + real_sin)
    return (real_cos + imag_sin, imag_cos - real_sin)


def left_apply(real_part, imag_part, tables, inverse):
    cosine, sines = tables
    real_cos = jnp.einsum("ij,...jk->...ik", cosine, real_part, precision=highest)
    real_sin = jnp.einsum("ij,...jk->...ik", sines, real_part, precision=highest)
    imag_cos = jnp.einsum("ij,...jk->...ik", cosine, imag_part, precision=highest)
    imag_sin = jnp.einsum("ij,...jk->...ik", sines, imag_part, precision=highest)
    if inverse:
        return (real_cos - imag_sin, imag_cos + real_sin)
    return (real_cos + imag_sin, imag_cos - real_sin)


def transform(real_part, imag_part, tables, inverse):
    half_re, half_im = right_apply(real_part, imag_part, tables, inverse)
    return left_apply(half_re, half_im, tables, inverse)


def complex_mul(left_re, left_im, right_re, right_im):
    return (left_re * right_re - left_im * right_im, left_re * right_im + left_im * right_re)


def position_terms(layers, measured, weights, probe_modes, kernel, tables):
    values = layers.astype(jnp.float32)
    one_re = values[:, 0, 0][:, None]
    one_im = values[:, 0, 1][:, None]
    two_re = values[:, 1, 0][:, None]
    two_im = values[:, 1, 1][:, None]
    probe_re = probe_modes[:, 0][None]
    probe_im = probe_modes[:, 1][None]
    kern_re, kern_im = kernel
    enter_re, enter_im = complex_mul(probe_re, probe_im, one_re, one_im)
    freq_re, freq_im = transform(enter_re, enter_im, tables, False)
    freq_re, freq_im = complex_mul(freq_re, freq_im, kern_re, kern_im)
    spread_re, spread_im = transform(freq_re, freq_im, tables, True)
    leave_re, leave_im = complex_mul(spread_re, spread_im, two_re, two_im)
    far_re, far_im = transform(leave_re, leave_im, tables, False)
    intensity = jnp.sum(far_re * far_re + far_im * far_im, axis=1, keepdims=True)
    factor = 1.0 - measured[:, None] / jnp.sqrt(jnp.maximum(intensity, 1.0))
    back_re, back_im = transform(far_re * factor, far_im * factor, tables, True)
    gtwo_re, gtwo_im = complex_mul(spread_re, -spread_im, back_re, back_im)
    bspread_re, bspread_im = complex_mul(two_re, -two_im, back_re, back_im)
    freq_re, freq_im = transform(bspread_re, bspread_im, tables, False)
    freq_re, freq_im = complex_mul(freq_re, freq_im, kern_re, -kern_im)
    bone_re, bone_im = transform(freq_re, freq_im, tables, True)
    gone_re, gone_im = complex_mul(probe_re, -probe_im, bone_re, bone_im)
    gprobe_re, gprobe_im = complex_mul(one_re, -one_im, bone_re, bone_im)
    slot_weight = weights.astype(jnp.float32)
    patch_weight = slot_weight[:, None, None, None, None]
    mode_weight = slot_weight[:, None, None, None]
    grad_one = jnp.stack([jnp.sum(gone_re, axis=1), jnp.sum(gone_im, axis=1)], axis=1)
    grad_two = jnp.stack([jnp.sum(gtwo_re, axis=1), jnp.sum(gtwo_im, axis=1)], axis=1)
    patch_grad = (jnp.stack([grad_one, grad_two], axis=1) * patch_weight).astype(jnp.bfloat16)
    probe_grad = jnp.stack(
        [jnp.sum(gprobe_re * mode_weight, axis=0), jnp.sum(gprobe_im * mode_weight, axis=0)], axis=1
    )
    return (patch_grad, probe_grad)


def run_slots(windows, measured, weights, probe_modes, kernel, tables):
    slot_count = windows.shape[0]
    group_size = math.gcd(slot_count, 4)
    rounds = slot_count // group_size
    grouped = (
        windows.reshape((rounds, group_size) + windows.shape[1:]),
        measured.reshape((rounds, group_size) + measured.shape[1:]),
        weights.reshape(rounds, group_size),
    )

    def one_group(members):
        group_windows, group_measured, group_weights = members

        def active(_):
            return position_terms(
                group_windows, group_measured, group_weights, probe_modes, kernel, tables
            )

        def nothing(_):
            return (
                jnp.zeros(group_windows.shape, jnp.bfloat16),
                jnp.zeros(probe_modes.shape, jnp.float32),
            )

        return lax.cond(jnp.any(group_weights > 0), active, nothing, 0)

    gradients, probe_parts = lax.map(one_group, grouped)
    return (gradients.reshape(windows.shape), jnp.sum(probe_parts, axis=0))


def split_bf16(values):
    high = values.astype(jnp.bfloat16)
    low = (values - high.astype(jnp.float32)).astype(jnp.bfloat16)
    return high, low


def stacked_tables(width):
    counter = np.arange(width)
    angles = (counter[:, None] * counter[None, :] % width) * (2.0 * np.pi / width)
    cosine = np.cos(angles) / np.sqrt(width)
    sines = np.sin(angles) / np.sqrt(width)
    forward = np.block([[cosine, -sines], [sines, cosine]])
    inverse = np.block([[cosine, sines], [-sines, cosine]])
    both = np.stack([forward, inverse])
    high = both.astype(jnp.bfloat16)
    low = (both - high.astype(np.float64)).astype(jnp.bfloat16)
    return jnp.asarray(np.stack([high, low], axis=1))


def split_dot(left, right, left_split, right_split):
    left_high, left_low = left_split(left)
    right_high, right_low = right_split(right)
    total = jnp.dot(left_high, right_high, preferred_element_type=jnp.float32)
    total = total + jnp.dot(left_low, right_high, preferred_element_type=jnp.float32)
    return total + jnp.dot(left_high, right_low, preferred_element_type=jnp.float32)


def position_kernel(rows_ref, window_ref, measured_ref, probe_ref, phase_ref, table_ref, patch_ref, probe_out_ref):
    width = measured_ref.shape[-1]
    modes = probe_ref.shape[0]

    @pl.when(pl.program_id(0) == 0)
    def _():
        probe_out_ref[...] = jnp.zeros(probe_out_ref.shape, jnp.float32)

    def table(index):
        return lambda _: (table_ref[index, 0], table_ref[index, 1])

    def transform(reals, imags, inverse):
        right_index = 1 if inverse else 0
        joined = jnp.concatenate(
            [jnp.concatenate([real, imag], axis=1) for real, imag in zip(reals, imags)], axis=0
        )
        half = split_dot(joined, None, split_bf16, table(right_index))
        stacked = jnp.concatenate(
            [
                jnp.concatenate(
                    [half[m * width:(m + 1) * width, :width], half[m * width:(m + 1) * width, width:]],
                    axis=0,
                )
                for m in range(len(reals))
            ],
            axis=1,
        )
        full = split_dot(None, stacked, table(1 - right_index), split_bf16)
        return (
            [full[:width, m * width:(m + 1) * width] for m in range(len(reals))],
            [full[width:, m * width:(m + 1) * width] for m in range(len(reals))],
        )

    def each(function, *lists):
        results = [function(*members) for members in zip(*lists)]
        return [r[0] for r in results], [r[1] for r in results]

    one_re = window_ref[0, 0, 0].astype(jnp.float32)
    one_im = window_ref[0, 0, 1].astype(jnp.float32)
    two_re = window_ref[0, 1, 0].astype(jnp.float32)
    two_im = window_ref[0, 1, 1].astype(jnp.float32)
    kern_re = phase_ref[0]
    kern_im = phase_ref[1]
    probe_re = [probe_ref[m, 0] for m in range(modes)]
    probe_im = [probe_ref[m, 1] for m in range(modes)]

    enter = each(lambda a, b: complex_mul(a, b, one_re, one_im), probe_re, probe_im)
    freq = transform(*enter, False)
    freq = each(lambda a, b: complex_mul(a, b, kern_re, kern_im), *freq)
    spread_re, spread_im = transform(*freq, True)
    leave = each(lambda a, b: complex_mul(a, b, two_re, two_im), spread_re, spread_im)
    far_re, far_im = transform(*leave, False)
    intensity = far_re[0] * far_re[0] + far_im[0] * far_im[0]
    for m in range(1, modes):
        intensity = intensity + far_re[m] * far_re[m] + far_im[m] * far_im[m]
    factor = 1.0 - measured_ref[0] / jnp.sqrt(jnp.maximum(intensity, 1.0))
    back_re, back_im = transform([f * factor for f in far_re], [f * factor for f in far_im], True)
    gtwo = each(lambda a, b, c, d: complex_mul(a, -b, c, d), spread_re, spread_im, back_re, back_im)
    bspread = each(lambda a, b: complex_mul(two_re, -two_im, a, b), back_re, back_im)
    freq = transform(*bspread, False)
    freq = each(lambda a, b: complex_mul(a, b, kern_re, -kern_im), *freq)
    bone_re, bone_im = transform(*freq, True)
    gone = each(lambda a, b, c, d: complex_mul(a, -b, c, d), probe_re, probe_im, bone_re, bone_im)
    for m in range(modes):
        term_re, term_im = complex_mul(one_re, -one_im, bone_re[m], bone_im[m])
        probe_out_ref[m, 0] = probe_out_ref[m, 0] + term_re
        probe_out_ref[m, 1] = probe_out_ref[m, 1] + term_im
    patch_ref[0, 0, 0] = sum(gone[0][1:], gone[0][0]).astype(patch_ref.dtype)
    patch_ref[0, 0, 1] = sum(gone[1][1:], gone[1][0]).astype(patch_ref.dtype)
    patch_ref[0, 1, 0] = sum(gtwo[0][1:], gtwo[0][0]).astype(patch_ref.dtype)
    patch_ref[0, 1, 1] = sum(gtwo[1][1:], gtwo[1][0]).astype(patch_ref.dtype)


def run_positions(arrived, rows, measured, probe_modes, phase_map):
    count, width = measured.shape[0], measured.shape[-1]
    modes = probe_modes.shape[0]
    tables = stacked_tables(width)
    phases = jnp.stack([jnp.cos(phase_map), jnp.sin(phase_map)])
    flops = count * modes * 6 * 2 * 3 * 2 * width * (2 * width) * (2 * width)
    row_block = (1,) + arrived.shape[1:]
    return pl.pallas_call(
        position_kernel,
        grid_spec=pltpu.PrefetchScalarGridSpec(
            num_scalar_prefetch=1,
            grid=(count,),
            in_specs=[
                pl.BlockSpec(row_block, lambda p, rows_ref: (rows_ref[p], 0, 0, 0, 0)),
                pl.BlockSpec((1, width, width), lambda p, rows_ref: (p, 0, 0)),
                pl.BlockSpec(probe_modes.shape, lambda p, rows_ref: (0, 0, 0, 0)),
                pl.BlockSpec(phases.shape, lambda p, rows_ref: (0, 0, 0)),
                pl.BlockSpec(tables.shape, lambda p, rows_ref: (0, 0, 0, 0)),
            ],
            out_specs=[
                pl.BlockSpec(row_block, lambda p, rows_ref: (rows_ref[p], 0, 0, 0, 0)),
                pl.BlockSpec(probe_modes.shape, lambda p, rows_ref: (0, 0, 0, 0)),
            ],
        ),
        out_shape=[
            jax.ShapeDtypeStruct(arrived.shape, jnp.bfloat16),
            jax.ShapeDtypeStruct(probe_modes.shape, jnp.float32),
        ],
        compiler_params=pltpu.CompilerParams(dimension_semantics=("arbitrary",)),
        cost_estimate=pl.CostEstimate(
            flops=flops, transcendentals=count * width * width, bytes_accessed=count * 6 * width * width * 4
        ),
    )(rows, arrived, measured, probe_modes, phases, tables)


def picker(size, extent, start, along_rows):
    if along_rows:
        small = lax.broadcasted_iota(jnp.int32, (size, extent), 0)
        large = lax.broadcasted_iota(jnp.int32, (size, extent), 1)
    else:
        small = lax.broadcasted_iota(jnp.int32, (extent, size), 1)
        large = lax.broadcasted_iota(jnp.int32, (extent, size), 0)
    return (large == small + start).astype(jnp.bfloat16)


def selectors(corners, width, extent):
    position = jnp.arange(width, dtype=jnp.int32)
    cells = jnp.arange(extent, dtype=jnp.int32)
    rows = cells[None, None, :] == corners[:, 0, None, None] + position[None, :, None]
    cols = cells[None, None, :] == corners[:, 1, None, None] + position[None, :, None]
    return rows.astype(jnp.bfloat16), cols.astype(jnp.bfloat16)


def cut_windows(local_tiles, corners, width):
    extent = local_tiles.shape[-1]
    rows, cols = selectors(corners, width, extent)
    picked_rows = jnp.einsum(
        "iar,skrc->iskac", rows, local_tiles, preferred_element_type=jnp.float32
    ).astype(jnp.bfloat16)
    return jnp.einsum(
        "iskac,ibc->iskab", picked_rows, cols, preferred_element_type=jnp.float32
    ).astype(jnp.bfloat16)


def accumulate_kernel(request_ref, grad_ref, out_ref):
    slices, parts, extent, _ = out_ref.shape
    width = grad_ref.shape[-1]
    out_ref[...] = jnp.zeros(out_ref.shape, jnp.float32)
    planes = [(s, q) for s in range(slices) for q in range(parts)]
    reach = width + 8
    span = 2 * width

    def add_slot(slot):
        top = request_ref[slot, 0]
        start = pl.multiple_of(jnp.minimum(top // 8 * 8, extent - reach), 8)
        shift = picker(width, reach, top - start, False)
        left = request_ref[slot, 1]
        first = pl.multiple_of(jnp.minimum(left // width * width, extent - span), width)
        cols = picker(width, span, left - first, True)
        stacked = jnp.concatenate([grad_ref[slot, s, q] for s, q in planes], axis=0)
        band = jnp.dot(stacked, cols, preferred_element_type=jnp.float32).astype(jnp.bfloat16)
        wide = jnp.concatenate([band[k * width:(k + 1) * width] for k in range(len(planes))], axis=1)
        placed = jnp.dot(shift, wide, preferred_element_type=jnp.float32)
        placed = jnp.where(request_ref[slot, 2] > 0, placed, jnp.zeros_like(placed))
        for k, (s, q) in enumerate(planes):
            out_ref[s, q, pl.ds(start, reach), pl.ds(first, span)] = (
                out_ref[s, q, pl.ds(start, reach), pl.ds(first, span)]
                + placed[:, k * span:(k + 1) * span]
            )

    def pair(index, carry):
        add_slot(2 * index)
        add_slot(2 * index + 1)
        return carry

    lax.fori_loop(0, grad_ref.shape[0] // 2, pair, 0)


def accumulate(gradients, requests, local_tiles):
    slices, parts, extent, _ = local_tiles.shape
    width = gradients.shape[-1]
    return pl.pallas_call(
        accumulate_kernel,
        in_specs=[
            pl.BlockSpec(memory_space=pltpu.SMEM),
            pl.BlockSpec(memory_space=pltpu.VMEM),
        ],
        out_specs=pl.BlockSpec(memory_space=pltpu.VMEM),
        out_shape=jax.ShapeDtypeStruct(local_tiles.shape, jnp.float32),
        cost_estimate=pl.CostEstimate(
            flops=8 * slices * parts * 2 * width * extent * (extent + width),
            transcendentals=0,
            bytes_accessed=gradients.size * 2 + local_tiles.size * 4,
        ),
    )(requests, gradients)


def on_device(object_tiles, probe_modes, phase_map, amplitudes, offsets, owners):
    tile_count = lax.axis_size("obj")
    position_count = amplitudes.shape[0]
    width = amplitudes.shape[1]
    capacity = max(2, 2 * position_count // tile_count)
    owner_ids = owners[:, 0]
    hits = (owner_ids[:, None] == jnp.arange(tile_count, dtype=jnp.int32)[None, :]).astype(
        jnp.int32
    )
    ranks = jnp.sum((jnp.cumsum(hits, axis=0) - 1) * hits, axis=1)
    destination = owner_ids * capacity + ranks
    buffer_rows = tile_count * capacity
    marked = jnp.concatenate([offsets, jnp.ones((position_count, 1), jnp.int32)], axis=1)
    request_send = jnp.zeros((buffer_rows, 3), jnp.int32).at[destination].set(marked)
    requests = lax.all_to_all(request_send, "obj", split_axis=0, concat_axis=0, tiled=True)
    windows = cut_windows(object_tiles, requests[:, :2], width)
    arrived = lax.all_to_all(windows, "obj", split_axis=0, concat_axis=0, tiled=True)
    grad_buffer, probe_part = run_positions(arrived, destination, amplitudes, probe_modes, phase_map)
    returned = lax.all_to_all(grad_buffer, "obj", split_axis=0, concat_axis=0, tiled=True)
    running = accumulate(returned, requests, object_tiles)
    probe_scan = lax.psum(probe_part, "scan")
    running, probe_scan = lax.optimization_barrier((running, probe_scan))
    tile_total = lax.psum(running, "scan")
    probe_chunks = probe_scan.reshape(tile_count, -1)
    probe_piece = jnp.sum(
        lax.all_to_all(probe_chunks, "obj", split_axis=0, concat_axis=0, tiled=True), axis=0
    )
    piece_total = jnp.broadcast_to(probe_piece[None], probe_chunks.shape)
    probe_total = lax.all_to_all(piece_total, "obj", split_axis=0, concat_axis=0, tiled=True)
    probe_total = probe_total.reshape(probe_part.shape)
    return (tile_total, probe_total)


def solution(mesh):
    placed = (
        P(None, None, "obj", None),
        P(),
        P(),
        P(("obj", "scan"), None, None),
        P(("obj", "scan"), None),
        P(("obj", "scan"), None),
    )
    return jax.shard_map(
        on_device,
        mesh=mesh,
        in_specs=placed,
        out_specs=(P(None, None, "obj", None), P()),
        check_vma=False,
    )
```
